256 devices in a mesh: ctx: 32 (over z_hi, x, y), fsdp: 8 (over z_lo, core).
Axes of the slice: x: 4, y: 4, z: 8 (z_hi: 2, z_lo: 4; z = z_hi * 4 + z_lo), core: 2. Of those that a mesh axis runs over, the one named last changes fastest.
Arguments:
- out_grad: bfloat16 [4096, 32768], P('fsdp', 'ctx'), may hold values from -6 to 6
- gate_values: bfloat16 [4096, 32768], P('fsdp', 'ctx'), may hold values from -6 to 6
- kv_product: bfloat16 [4096, 32768], P('fsdp', 'ctx'), may hold values from -6 to 6
- w_out: bfloat16 [4096, 4096], P('ctx', 'fsdp'), may hold values from -0.09375 to 0.09375
- filters: bfloat16 [8, 32, 16, 128], P('fsdp', 'ctx'), may hold values from -0.5 to 0.5
Outputs:
- gate_grad: float32 [4096, 32768], P('fsdp', 'ctx')
- kv_grad: bfloat16 [4096, 32768], P('fsdp', 'ctx')
- filter_grad: float32 [8, 32, 16, 128], P('fsdp', 'ctx')
- w_grad: float32 [4096, 4096], P('ctx', 'fsdp')
The draws below stay inside these ranges and needn't reach their ends.
All inputs are finite; a program needn't handle non-finite values.
Results may differ from the reference program's by a relative error of at most 0.0049.
Values may be sent and summed in bfloat16 or wider, within the bound.
A program may use at most 128 MiB of HBM per device.

```python
import math
import jax
import jax.numpy as jnp
from jax import lax

D = 4096
TAPS = 128
TOKENS = 32768
CPD = 16
N_CTX = 32
N_FSDP = 8


def with_spikes(array, stream_key, source, target, parts, factor):
    owner, partner = [(jnp.arange(array.shape[dim]) // (array.shape[dim] // parts)).reshape([-1 if axis == dim else 1 for axis in range(array.ndim)]) for dim in (source, target)]
    chosen = jax.random.permutation(stream_key, parts)[partner]
    strong = (owner == chosen) | (owner == (partner + parts // 2) % parts)
    return jnp.where(strong, factor * array, array)


def level_of(key, shape, cuts, least, high):
    def one(axis_at, blocks):
        draws = jax.random.uniform(jax.random.fold_in(jax.random.fold_in(key, 6), axis_at), (blocks,), jnp.float32, least / len(cuts), high / len(cuts))
        return jnp.repeat(jnp.exp(draws), shape[axis_at] // blocks).reshape((-1,) + (1,) * (len(shape) - axis_at - 1))

    gain = one(*cuts[0])
    for cut in cuts[1:]:
        gain = gain * one(*cut)
    return gain


def gaussian(rng, shape, scale, bound, split=(), held_as=jnp.bfloat16):
    drawn = scale * jax.random.normal(rng, shape, jnp.float32)
    if split:
        drawn = drawn * level_of(rng, shape, split, -0.22, 0.18)
    return jnp.clip(drawn, -bound, bound).astype(held_as)


def gaussian_with(rng, shape, deviation, most, cuts, heavy, held_as=jnp.bfloat16):
    array = deviation * jax.random.normal(rng, shape, jnp.float32)
    if cuts:
        array = array * level_of(rng, shape, cuts, -0.22, 0.18)
    return jnp.clip(with_spikes(array, jax.random.fold_in(rng, 3), *heavy), -most, most).astype(held_as)


def setup_inputs(seed: int = 0) -> dict:
    key_of = jax.random.split(jax.random.key(seed), 6)
    out_grad = gaussian_with(key_of[0], (D, TOKENS), 1.0, 6.0, ((0, 8), (1, 32)), (1, 0, 32, 2.75))
    gate_values = gaussian(key_of[1], (D, TOKENS), 1.0, 6.0, ((0, 8), (1, 32)))
    kv_product = gaussian(key_of[2], (D, TOKENS), 1.0, 6.0, ((0, 8), (1, 32)))
    w_out = gaussian(key_of[3], (D, D), D ** -0.5, 0.09375, ((0, 32), (1, 8)))
    filters = gaussian(key_of[4], (N_FSDP, N_CTX, CPD, TAPS), TAPS ** -0.5, 0.5, ((0, 8), (1, 32)))
    return {"out_grad": out_grad, "gate_values": gate_values, "kv_product": kv_product, "w_out": w_out, "filters": filters}


exact_mode = lax.Precision.HIGHEST

def toeplitz_pair(filters):
    tap_count = filters.shape[1]
    offset = jnp.arange(tap_count)[None, :] - jnp.arange(tap_count)[:, None]
    lower_take = jnp.take(filters, jnp.where(offset >= 0, offset, 0), axis=1)
    near_band = jnp.where(offset >= 0, lower_take, 0.0)
    upper_take = jnp.take(filters, jnp.where(offset < 0, offset + tap_count, 0), axis=1)
    far_band = jnp.where(offset < 0, upper_take, 0.0)
    return (near_band, far_band)

def causal_mix(filters, signal):
    channels, seq_len = signal.shape
    tap_count = filters.shape[1]
    near_band, far_band = toeplitz_pair(filters)
    current = signal.reshape(channels, seq_len // tap_count, tap_count)
    previous = jnp.concatenate([jnp.zeros((channels, 1, tap_count), signal.dtype), current[:, :-1]], axis=1)
    result = jnp.einsum('cbs,csr->cbr', current, near_band, precision=exact_mode)
    result = result + jnp.einsum('cbs,csr->cbr', previous, far_band, precision=exact_mode)
    return result.reshape(channels, seq_len)

def channel_block(block_args):
    filters, signal, cotangent = block_args
    mixed, pullback = jax.vjp(causal_mix, filters, signal)
    filter_part, signal_grad = pullback(cotangent)
    return (mixed, signal_grad, filter_part)

def reference(out_grad, gate_values, kv_product, w_out, filters):
    mix_grad = jnp.dot(w_out.T, out_grad, preferred_element_type=jnp.float32)
    conv_grad = (mix_grad * gate_values.astype(jnp.float32)).astype(jnp.bfloat16)
    groups = D // 128
    flat_filters = filters.astype(jnp.float32).reshape(groups, 128, TAPS)
    signal = kv_product.astype(jnp.float32).reshape(groups, 128, TOKENS)
    cotangent = conv_grad.astype(jnp.float32).reshape(groups, 128, TOKENS)
    mixed, signal_grad, filter_part = lax.map(channel_block, (flat_filters, signal, cotangent))
    mixed = mixed.reshape(D, TOKENS).astype(jnp.bfloat16)
    kv_grad = signal_grad.reshape(D, TOKENS).astype(jnp.bfloat16)
    norm_scale = 1.0 / math.sqrt(TOKENS)
    filter_grad = filter_part.reshape(filters.shape) * norm_scale
    mixed_wide = mixed.astype(jnp.float32)
    gate_grad = mix_grad * mixed_wide
    gated_rows = (gate_values.astype(jnp.float32) * mixed_wide).astype(jnp.bfloat16)
    w_grad = jnp.dot(out_grad, gated_rows.T, preferred_element_type=jnp.float32) * norm_scale
    return (gate_grad, kv_grad, filter_grad, w_grad)
```

```python
import functools
import math

import jax
import jax.numpy as jnp
from jax import lax
from jax.experimental import pallas as pl
from jax.experimental.pallas import tpu as pltpu
from jax.sharding import PartitionSpec as P

F32 = jnp.float32
BF = jnp.bfloat16

def band_pair(row):
    rows = lax.broadcasted_iota(jnp.int32, (128, 128), 0)
    lanes = lax.broadcasted_iota(jnp.int32, (128, 128), 1)
    turned = pltpu.roll(jnp.broadcast_to(row, (128, 128)), 0, 1, stride=1, stride_axis=0)
    near = jnp.where(lanes >= rows, turned, 0.0).astype(BF)
    far = jnp.where(lanes < rows, turned, 0.0).astype(BF)
    return far, near

def conv_group(h16, lhs, swap):
    sub = lax.broadcasted_iota(jnp.int32, (8, 128), 0)
    out = [[None, None] for _ in range(8)]
    for pair in range(8):
        cols = []
        for ch in (2 * pair, 2 * pair + 1):
            far, near = band_pair(h16[ch:ch + 1, :])
            cols.append(jnp.concatenate([far, near] if not swap else [near, far], axis=0))
        w = jnp.concatenate(cols, axis=1)
        r = jnp.dot(lhs, w, preferred_element_type=F32)
        for k in range(2):
            ch = 2 * pair + k
            half = ch // 8
            for b in range(8):
                piece = r[b * 16 + half * 8: b * 16 + half * 8 + 8, k * 128:(k + 1) * 128]
                o = out[b][half]
                out[b][half] = piece if o is None else jnp.where(sub == ch % 8, piece, o)
    return [jnp.concatenate(o, axis=0) for o in out]

def kernel_a(kv_ref, halo_ref, gate_ref, filt_ref, mixed_ref, gated_ref):
    def body(g, _):
        rows = pl.ds(pl.multiple_of(g * 16, 16), 16)
        xs = [halo_ref[rows, :]] + [kv_ref[rows, b * 128:(b + 1) * 128] for b in range(8)]
        lhs = jnp.concatenate([jnp.concatenate([xs[b], xs[b + 1]], axis=1) for b in range(8)], axis=0)
        outs = conv_group(filt_ref[rows, :].astype(F32), lhs, False)
        for b in range(8):
            m = outs[b].astype(BF)
            mixed_ref[rows, b * 128:(b + 1) * 128] = m
            gated_ref[rows, b * 128:(b + 1) * 128] = (gate_ref[rows, b * 128:(b + 1) * 128].astype(F32) * m.astype(F32)).astype(BF)
        return 0
    lax.fori_loop(0, 32, body, 0)

def conv_a(kv, halo, gate, filt):
    return pl.pallas_call(kernel_a, out_shape=[jax.ShapeDtypeStruct(kv.shape, BF)] * 2,
        in_specs=[pl.BlockSpec(memory_space=pltpu.VMEM)] * 4, out_specs=[pl.BlockSpec(memory_space=pltpu.VMEM)] * 2,
        compiler_params=pltpu.CompilerParams(vmem_limit_bytes=48 << 20))(kv, halo, gate, filt)

def kernel_b(kv_ref, halo_ref, cg_ref, after_ref, rfilt_ref, kvg_ref, fg_ref, part):
    rows_i = lax.broadcasted_iota(jnp.int32, (128, 128), 0)
    lanes_i = lax.broadcasted_iota(jnp.int32, (128, 128), 1)
    def body(g, _):
        rows = pl.ds(pl.multiple_of(g * 16, 16), 16)
        xs = [halo_ref[rows, :]] + [kv_ref[rows, b * 128:(b + 1) * 128] for b in range(8)]
        gs = [cg_ref[rows, b * 128:(b + 1) * 128] for b in range(8)] + [after_ref[rows, :]]
        lhs = jnp.concatenate([jnp.concatenate([gs[b], gs[b + 1]], axis=1) for b in range(8)], axis=0)
        hr = rfilt_ref[rows, :].astype(F32)
        sub = lax.broadcasted_iota(jnp.int32, (8, 128), 0)
        out = [[None, None] for _ in range(8)]
        x = jnp.concatenate([jnp.concatenate([xs[b], xs[b + 1]], axis=1) for b in range(8)], axis=0)
        xt = x.astype(F32).T.astype(BF)
        gg = jnp.concatenate(gs[:8], axis=0)
        chan = lax.broadcasted_iota(jnp.int32, (128, 128), 0) % 16
        ggf = gg.astype(F32)
        for pair in range(8):
            cols = []; gcols = []
            for ch in (2 * pair, 2 * pair + 1):
                turned = pltpu.roll(jnp.broadcast_to(hr[ch:ch + 1, :], (128, 128)), 0, 1, stride=1, stride_axis=0)
                near = jnp.where(rows_i >= lanes_i, turned, 0.0).astype(BF)
                far = jnp.where(rows_i < lanes_i, turned, 0.0).astype(BF)
                cols.append(jnp.concatenate([near, far], axis=0))
                gcols.append(jnp.where(chan == ch, ggf, 0.0).astype(BF))
            r = jnp.dot(lhs, jnp.concatenate(cols, axis=1), preferred_element_type=F32)
            q = jnp.dot(xt, jnp.concatenate(gcols, axis=1), preferred_element_type=F32)
            for k in range(2):
                ch = 2 * pair + k
                half = ch // 8
                for b in range(8):
                    piece = r[b * 16 + half * 8: b * 16 + half * 8 + 8, k * 128:(k + 1) * 128]
                    o = out[b][half]
                    out[b][half] = piece if o is None else jnp.where(sub == ch % 8, piece, o)
                n = jnp.where(lanes_i >= rows_i, q[128:, k * 128:(k + 1) * 128], q[:128, k * 128:(k + 1) * 128])
                acc = n[0:8]
                for v in range(1, 16):
                    acc = acc + pltpu.roll(n[8 * v:8 * v + 8], 128 - 8 * v, 1)
                part[ch] = acc
        for b in range(8):
            kvg_ref[rows, b * 128:(b + 1) * 128] = jnp.concatenate(out[b], axis=0).astype(BF)
        fg = part[:, 0, :]
        for u in range(1, 8):
            fg = fg + pltpu.roll(part[:, u, :], 128 - u, 1)
        fg_ref[rows, :] = fg
        return 0
    lax.fori_loop(0, 32, body, 0)

def conv_b(kv, halo, cg, after, rfilt):
    return pl.pallas_call(kernel_b, out_shape=[jax.ShapeDtypeStruct(kv.shape, BF), jax.ShapeDtypeStruct((kv.shape[0], 128), F32)],
        in_specs=[pl.BlockSpec(memory_space=pltpu.VMEM)] * 5, out_specs=[pl.BlockSpec(memory_space=pltpu.VMEM)] * 2,
        scratch_shapes=[pltpu.VMEM((16, 8, 128), F32)],
        compiler_params=pltpu.CompilerParams(vmem_limit_bytes=48 << 20))(kv, halo, cg, after, rfilt)


NCH = 2


def remote(src, dst, send, recv, **where):
    return pltpu.make_async_remote_copy(src, dst, send, recv, device_id=where, device_id_type=pl.DeviceIdType.MESH)


def exchange_kernel(
    g_ref, wt_ref, gated_ref, gate_ref, mixed_ref,
    gate_grad_ref, conv_ref, after_ref, w_grad_ref,
    gbuf, wbuf, gated_t, prod, mix, head, after,
    y1s, y1b, y2s, y2b, x1s, x1b, x2s, x2b, zs, zb,
    g_send, g_recv, s_send, s_recv, w_send, w_recv,
    y1_send, y1_recv, y2_send, y2_recv, x1_send, x1_recv, x2_send, x2_recv, z_send, z_recv,
    h_send, h_recv, l_sem, *, scale,
):
    c = lax.axis_index("ctx")
    f = lax.axis_index("fsdp")
    z, k = f // 2, f % 2
    zh, x, y = c // 16, (c // 4) % 4, c % 4
    xy = c % 16
    right, left, twin = f + 2, f - 2, f + 1 - 2 * k
    partner = (c + 16) % 32

    def at_y(d):
        return c - y + (y + d) % 4

    def at_x(d):
        return c + 4 * ((x + d) % 4 - x)

    barrier = pltpu.get_barrier_semaphore()

    def greet(**where):
        pl.semaphore_signal(barrier, inc=1, device_id=where, device_id_type=pl.DeviceIdType.MESH)

    @pl.when(z < 3)
    def _():
        greet(fsdp=right)

    @pl.when(z > 0)
    def _():
        greet(fsdp=left)

    greet(fsdp=twin)
    for d in (1, 2, 3):
        greet(ctx=at_y(d))
    greet(ctx=at_x(1))
    greet(ctx=at_x(3))
    greet(ctx=partner)

    @pl.when(c < 31)
    def _():
        greet(ctx=c + 1)

    @pl.when(c > 0)
    def _():
        greet(ctx=c - 1)

    own_g = pltpu.make_async_copy(g_ref, gbuf.at[f], l_sem.at[0])
    own_w = pltpu.make_async_copy(wt_ref, wbuf.at[xy, zh], l_sem.at[1])
    own_g.start()
    own_w.start()
    count = jnp.where(z < 3, 1, 0) + jnp.where(z > 0, 1, 0) + jnp.where(c < 31, 1, 0) + jnp.where(c > 0, 1, 0) + 7
    pl.semaphore_wait(barrier, count)
    own_g.wait()
    own_w.wait()

    span = 512 // NCH

    def g_copy(p, ch, way):
        block = gbuf.at[2 * p + k, pl.ds(ch * span, span)]
        to = right if way == 0 else left
        return remote(block, block, g_send.at[p, ch, way], g_recv.at[p, ch], fsdp=to)

    def twin_copy(p, ch):
        block = gbuf.at[2 * p + k, pl.ds(ch * span, span)]
        return remote(block, block, s_send.at[p, ch], s_recv.at[p, ch], fsdp=twin)

    def wz_copy():
        block = wbuf.at[xy, zh]
        return remote(block, block, w_send.at[0], w_recv.at[0], ctx=partner)

    def wy_copy(d):
        block = wbuf.at[xy]
        return remote(block, block, w_send.at[d], w_recv.at[d], ctx=at_y(d))

    def wx_copy(d):
        block = wbuf.at[pl.ds(4 * x, 4)]
        return remote(block, block, w_send.at[4 + d], w_recv.at[4 + d], ctx=at_x(d))

    def wf_copy(d):
        block = wbuf.at[pl.ds(4 * ((x - d) % 4) + (0 if d == 1 else 2), 2)]
        return remote(block, block, w_send.at[8 + d], w_recv.at[8 + d], ctx=at_x(d))

    wz_copy().start()
    for ch in range(NCH):
        @pl.when(z < 3)
        def _():
            g_copy(z, ch, 0).start()

        @pl.when(z > 0)
        def _():
            g_copy(z, ch, 1).start()

        twin_copy(z, ch).start()

    mix[...] = jnp.zeros_like(mix)

    def turn(i, carry):
        rows = pl.ds(pl.multiple_of(i * 128, 128), 128)
        gated_t[:, rows] = gated_ref[rows, :].astype(F32).T.astype(BF)
        return carry

    for i in range(4):
        turn(i, 0)

    wz_copy().wait_recv()
    for d in (1, 3, 2):
        wy_copy(d).start()
    for d in (1, 3, 2):
        wy_copy(d).wait_recv()
    for d in (1, 3):
        wx_copy(d).start()

    def y1_copy(b, j):
        return remote(y1s.at[b, j], y1b.at[b, j], y1_send.at[b, j], y1_recv.at[b, j], ctx=at_y(1 if j == 0 else 3))

    def y2_copy(b, j):
        return remote(y2s.at[b, j], y2b.at[b, j], y2_send.at[b, j], y2_recv.at[b, j], ctx=at_y(1 if j == 0 else 3))

    def x1_copy(b, j):
        return remote(x1s.at[b, j], x1b.at[b, j], x1_send.at[b, j], x1_recv.at[b, j], ctx=at_x(1 if j == 0 else 3))

    def x2_copy(b, j):
        return remote(x2s.at[b], x2b.at[b, j], x2_send.at[b], x2_recv.at[b, j], ctx=at_x(1 if j == 0 else 3))

    def z_copy():
        return remote(zs, zb, z_send, z_recv, ctx=partner)

    def multiply_rows(p):
        def tile(i, carry):
            b, h = 2 * p + i // 2, i % 2
            lhs = gbuf[b, pl.ds(pl.multiple_of(h * 256, 256), 256), :]
            part = jnp.dot(lhs, gated_t[...], preferred_element_type=F32)
            prod[b, pl.ds(2 * h, 2)] = part.reshape(2, 128, 512)
            return carry

        lax.fori_loop(0, 4, tile, 0)
        for i in range(2):
            b = 2 * p + i
            far = prod[b, (y + 2) % 4].astype(BF)
            y1s[b, 0] = far[:, :256]
            y1s[b, 1] = far[:, 256:]
            for j in range(2):
                y1_copy(b, j).start()

    def multiply_columns(p):
        def tile(i, carry):
            b, h, n = 2 * p + i // 4, (i // 2) % 2, i % 2
            rows = pl.ds(pl.multiple_of(h * 256, 256), 256)
            cols = pl.ds(pl.multiple_of(n * 512, 512), 512)
            lhs = jnp.concatenate([wbuf[4 * (b % 4) + q, b // 4, rows, :] for q in range(4)], axis=1)
            mix[rows, cols] += jnp.dot(lhs, gbuf[b, :, cols], preferred_element_type=F32)
            return carry

        lax.fori_loop(0, 8, tile, 0)

    def round_y2(p):
        for i in range(2):
            b = 2 * p + i
            y1_copy(b, 0).wait_recv()
            up = prod[b, (y + 1) % 4]
            y2s[b, 0, :, :256] = (up[:, :256] + y1b[b, 0].astype(F32)).astype(BF)
            y2s[b, 0, :, 256:] = up[:, 256:].astype(BF)
            y2_copy(b, 0).start()
            y1_copy(b, 1).wait_recv()
            down = prod[b, (y + 3) % 4]
            y2s[b, 1, :, :256] = down[:, :256].astype(BF)
            y2s[b, 1, :, 256:] = (down[:, 256:] + y1b[b, 1].astype(F32)).astype(BF)
            y2_copy(b, 1).start()

    def round_x1(p):
        for i in range(2):
            b = 2 * p + i
            y2_copy(b, 0).wait_recv()
            y2_copy(b, 1).wait_recv()
            total = prod[b, y] + y2b[b, 0].astype(F32) + y2b[b, 1].astype(F32)
            prod[b, y] = total

            @pl.when((x - b) % 4 == 2)
            def _():
                x1s[b, 0] = total[:, :256].astype(BF)
                x1s[b, 1] = total[:, 256:].astype(BF)
                for j in range(2):
                    x1_copy(b, j).start()

    def round_x2(p):
        for i in range(2):
            b = 2 * p + i
            role = (x - b) % 4

            @pl.when(role == 3)
            def _():
                x1_copy(b, 0).wait_recv()
                x2s[b, :, :256] = (prod[b, y, :, :256] + x1b[b, 0].astype(F32)).astype(BF)
                x2s[b, :, 256:] = prod[b, y, :, 256:].astype(BF)
                x2_copy(b, 0).start()

            @pl.when(role == 1)
            def _():
                x1_copy(b, 1).wait_recv()
                x2s[b, :, :256] = prod[b, y, :, :256].astype(BF)
                x2s[b, :, 256:] = (prod[b, y, :, 256:] + x1b[b, 1].astype(F32)).astype(BF)
                x2_copy(b, 1).start()

    def round_z(p):
        for i in range(2):
            b = 2 * p + i

            @pl.when((x - b) % 4 == 0)
            def _():
                x2_copy(b, 0).wait_recv()
                x2_copy(b, 1).wait_recv()
                total = prod[b, y] + x2b[b, 0].astype(F32) + x2b[b, 1].astype(F32)

                @pl.when(b // 4 == zh)
                def _():
                    prod[b, y] = total

                @pl.when(b // 4 != zh)
                def _():
                    zs[...] = total.astype(BF)
                    z_copy().start()

    def sides(s, act):
        @pl.when(z >= s)
        def _():
            act(z - s)

        @pl.when((s > 0) & (z + s < 4))
        def _():
            act(z + s)

    def step(s, carry):
        for ch in range(NCH):
            @pl.when((s > 0) & (z >= s))
            def _():
                g_copy(z - s, ch, 0).wait_recv()

                @pl.when(z < 3)
                def _():
                    g_copy(z - s, ch, 0).start()

                twin_copy(z - s, ch).start()

            @pl.when((s > 0) & (z + s < 4))
            def _():
                g_copy(z + s, ch, 1).wait_recv()

                @pl.when(z > 0)
                def _():
                    g_copy(z + s, ch, 1).start()

                twin_copy(z + s, ch).start()

        def arrive(p):
            for ch in range(NCH):
                twin_copy(p, ch).wait_recv()
            multiply_rows(p)

        sides(s, arrive)

        @pl.when(s > 0)
        def _():
            sides(s - 1, round_x2)

        @pl.when(s == 1)
        def _():
            wx_copy(1).wait_recv()
            wf_copy(1).start()
            wx_copy(3).wait_recv()
            wf_copy(3).start()

        @pl.when(s == 2)
        def _():
            wf_copy(1).wait_recv()
            wf_copy(3).wait_recv()

        @pl.when(s >= 2)
        def _():
            def late(q, carry):
                sides(q, multiply_columns)
                return carry

            lax.fori_loop(jnp.where(s == 2, 0, 3), s + 1, late, 0)

        sides(s, round_y2)

        @pl.when(s > 0)
        def _():
            sides(s - 1, round_z)

        sides(s, round_x1)
        return carry

    lax.fori_loop(0, 4, step, 0)

    def finish(i, carry):
        rows = pl.ds(pl.multiple_of(i * 32, 32), 32)
        wide = mix[rows, :]
        gate_grad_ref[rows, :] = wide * mixed_ref[rows, :].astype(F32)
        conv = (wide * gate_ref[rows, :].astype(F32)).astype(BF)
        conv_ref[rows, :] = conv
        head[rows, :] = conv[:, :128]
        return carry

    lax.fori_loop(0, 16, finish, 0)

    def h_copy():
        return remote(head, after, h_send, h_recv, ctx=c - 1)

    @pl.when(c > 0)
    def _():
        h_copy().start()

    sides(3, round_x2)
    sides(3, round_z)

    @pl.when(c < 31)
    def _():
        h_copy().wait_recv()
        after_ref[...] = after[...]

    @pl.when(c == 31)
    def _():
        after_ref[...] = jnp.zeros_like(after_ref)

    z_copy().wait_recv()
    w_grad_ref[...] = (prod[4 * zh + x, y] + zb[...].astype(F32)) * scale

    def sent_blocks(p, carry):
        for ch in range(NCH):
            @pl.when((p <= z) & (z < 3))
            def _():
                g_copy(p, ch, 0).wait_send()

            @pl.when((p >= z) & (z > 0))
            def _():
                g_copy(p, ch, 1).wait_send()

            twin_copy(p, ch).wait_send()
        return carry

    lax.fori_loop(0, 4, sent_blocks, 0)

    def sent_sums(b, carry):
        for j in range(2):
            y1_copy(b, j).wait_send()
            y2_copy(b, j).wait_send()
        role = (x - b) % 4

        @pl.when(role == 2)
        def _():
            for j in range(2):
                x1_copy(b, j).wait_send()

        @pl.when(role % 2 == 1)
        def _():
            x2_copy(b, 0).wait_send()

        return carry

    lax.fori_loop(0, 8, sent_sums, 0)
    z_copy().wait_send()
    wz_copy().wait_send()
    for d in (1, 2, 3):
        wy_copy(d).wait_send()
    for d in (1, 3):
        wx_copy(d).wait_send()
        wf_copy(d).wait_send()

    @pl.when(c > 0)
    def _():
        h_copy().wait_send()


def exchange(out_grad, wt, gated, gate, mixed, scale):
    vmem = pl.BlockSpec(memory_space=pltpu.VMEM)
    dma = pltpu.SemaphoreType.DMA
    return pl.pallas_call(
        functools.partial(exchange_kernel, scale=scale),
        out_shape=[
            jax.ShapeDtypeStruct((512, 1024), F32),
            jax.ShapeDtypeStruct((512, 1024), BF),
            jax.ShapeDtypeStruct((512, 128), BF),
            jax.ShapeDtypeStruct((128, 512), F32),
        ],
        in_specs=[vmem] * 5,
        out_specs=[vmem] * 4,
        scratch_shapes=[
            pltpu.VMEM((8, 512, 1024), BF),
            pltpu.VMEM((16, 2, 512, 128), BF),
            pltpu.VMEM((1024, 512), BF),
            pltpu.VMEM((8, 4, 128, 512), F32),
            pltpu.VMEM((512, 1024), F32),
            pltpu.VMEM((512, 128), BF),
            pltpu.VMEM((512, 128), BF),
            pltpu.VMEM((8, 2, 128, 256), BF),
            pltpu.VMEM((8, 2, 128, 256), BF),
            pltpu.VMEM((8, 2, 128, 512), BF),
            pltpu.VMEM((8, 2, 128, 512), BF),
            pltpu.VMEM((8, 2, 128, 256), BF),
            pltpu.VMEM((8, 2, 128, 256), BF),
            pltpu.VMEM((8, 128, 512), BF),
            pltpu.VMEM((8, 2, 128, 512), BF),
            pltpu.VMEM((128, 512), BF),
            pltpu.VMEM((128, 512), BF),
            dma((4, NCH, 2)), dma((4, NCH)), dma((4, NCH)), dma((4, NCH)), dma((12,)), dma((12,)),
            dma((8, 2)), dma((8, 2)), dma((8, 2)), dma((8, 2)), dma((8, 2)), dma((8, 2)), dma((8,)), dma((8, 2)),
            dma, dma, dma, dma, dma((2,)),
        ],
        compiler_params=pltpu.CompilerParams(
            collective_id=0, has_side_effects=True, vmem_limit_bytes=60 << 20
        ),
    )(out_grad, wt, gated, gate, mixed)


def on_device(out_grad, gate_values, kv_product, w_out, filters):
    ctx_count = lax.axis_size("ctx")
    norm_scale = 1.0 / math.sqrt(ctx_count * out_grad.shape[1])
    own_filters = filters.reshape(filters.shape[2:])
    taps = lax.all_gather(own_filters, "ctx", axis=0, tiled=True)
    before = lax.ppermute(kv_product[:, -128:], "ctx", [(i, i + 1) for i in range(ctx_count - 1)])
    mixed, gated = conv_a(kv_product, before, gate_values, taps)
    gate_grad, conv_grad, after, w_grad = exchange(out_grad, w_out.T, gated, gate_values, mixed, norm_scale)
    turned = jnp.roll(taps[:, ::-1], 1, axis=1)
    kv_grad, filter_part = conv_b(kv_product, before, conv_grad, after, turned)
    filter_grad = lax.psum_scatter(filter_part, "ctx", scatter_dimension=0, tiled=True) * norm_scale
    return (gate_grad, kv_grad, filter_grad.reshape(filters.shape), w_grad)


def solution(mesh):
    in_specs = (
        P("fsdp", "ctx"),
        P("fsdp", "ctx"),
        P("fsdp", "ctx"),
        P("ctx", "fsdp"),
        P("fsdp", "ctx", None, None),
    )
    out_specs = (P("fsdp", "ctx"), P("fsdp", "ctx"), P("fsdp", "ctx", None, None), P("ctx", "fsdp"))
    return jax.shard_map(
        on_device, mesh=mesh, in_specs=in_specs, out_specs=out_specs, check_vma=False
    )
```

```python
import functools
import math

import jax
import jax.numpy as jnp
from jax import lax
from jax.experimental import pallas as pl
from jax.experimental.pallas import tpu as pltpu
from jax.sharding import PartitionSpec as P

F32 = jnp.float32
BF = jnp.bfloat16


def bands(row):
    rows = lax.broadcasted_iota(jnp.int32, (128, 128), 0)
    lanes = lax.broadcasted_iota(jnp.int32, (128, 128), 1)
    turned = pltpu.roll(jnp.broadcast_to(row, (128, 128)), 0, 1, stride=1, stride_axis=0)
    near = jnp.where(lanes >= rows, turned, 0.0).astype(BF)
    far = jnp.where(lanes < rows, turned, 0.0).astype(BF)
    return far, near


def stack_blocks(parts):
    return jnp.concatenate(
        [jnp.concatenate([parts[b], parts[b + 1]], axis=1) for b in range(8)], axis=0
    )


def keep_own(out, product, ch, column):
    sub = lax.broadcasted_iota(jnp.int32, (8, 128), 0)
    half = ch // 8
    for b in range(8):
        start = b * 16 + half * 8
        piece = product[start : start + 8, column * 128 : (column + 1) * 128]
        old = out[b][half]
        out[b][half] = piece if old is None else jnp.where(sub == ch % 8, piece, old)


def conv_group(taps, lhs, _):
    out = [[None, None] for _ in range(8)]
    for pair in range(8):
        cols = [jnp.concatenate(bands(taps[ch : ch + 1, :]), axis=0) for ch in (2 * pair, 2 * pair + 1)]
        product = jnp.dot(lhs, jnp.concatenate(cols, axis=1), preferred_element_type=F32)
        for i in range(2):
            keep_own(out, product, 2 * pair + i, i)
    return [jnp.concatenate(o, axis=0) for o in out]


def back_group(before, kv, grad, after, rows, taps, part):
    xs = [before[rows, :]] + [kv[rows, b * 128 : (b + 1) * 128] for b in range(8)]
    gs = [grad[rows, b * 128 : (b + 1) * 128] for b in range(8)] + [after[rows, :]]
    row_at = lax.broadcasted_iota(jnp.int32, (128, 128), 0)
    lane_at = lax.broadcasted_iota(jnp.int32, (128, 128), 1)
    lhs = stack_blocks(gs)
    x_turned = stack_blocks(xs).astype(F32).T.astype(BF)
    wide = jnp.concatenate(gs[:8], axis=0).astype(F32)
    out = [[None, None] for _ in range(8)]
    for pair in range(8):
        band_rows, own_grad = [], []
        for ch in (2 * pair, 2 * pair + 1):
            far, near = bands(taps[ch : ch + 1, :])
            band_rows.append(jnp.concatenate([near, far], axis=1))
            own_grad.append(jnp.where(row_at % 16 == ch, wide, 0.0).astype(BF))
        product = lax.dot_general(
            lhs, jnp.concatenate(band_rows, axis=0), (((1,), (1,)), ((), ())), preferred_element_type=F32
        )
        outer = jnp.dot(x_turned, jnp.concatenate(own_grad, axis=1), preferred_element_type=F32)
        for i in range(2):
            ch = 2 * pair + i
            keep_own(out, product, ch, i)
            cols = slice(i * 128, (i + 1) * 128)
            both = jnp.where(lane_at >= row_at, outer[128:, cols], outer[:128, cols])
            acc = both[0:8]
            for v in range(1, 16):
                acc = acc + pltpu.roll(both[8 * v : 8 * v + 8], 128 - 8 * v, 1)
            part[ch] = acc
    taps_part = part[:, 0, :]
    for u in range(1, 8):
        taps_part = taps_part + pltpu.roll(part[:, u, :], 128 - u, 1)
    return [jnp.concatenate(o, axis=0) for o in out], taps_part


NCH = 2


def remote(src, dst, send, recv, **where):
    return pltpu.make_async_remote_copy(src, dst, send, recv, device_id=where, device_id_type=pl.DeviceIdType.MESH)


def exchange_kernel(
    g_ref, w_ref, gate_hbm, kv_hbm, filt_ref,
    gate_grad_ref, kv_grad_ref, filt_grad_ref, w_grad_ref,
    gbuf, wbuf, gated_t, prod, mix, head, after, tail, before, taps,
    gate, kv, mixed, work, part, fsum, fy, fx, fz, fxs, fzs,
    y1s, y1b, y2s, y2b, x1s, x1b, x2s, x2b, zs, zb,
    g_send, g_recv, s_send, s_recv, w_send, w_recv,
    y1_send, y1_recv, y2_send, y2_recv, x1_send, x1_recv, x2_send, x2_recv, z_send, z_recv,
    h_send, h_recv, b_send, b_recv, t_send, t_recv, f_send, f_recv, l_sem, *, scale,
):
    c = lax.axis_index("ctx")
    f = lax.axis_index("fsdp")
    z, k = f // 2, f % 2
    zh, x, y = c // 16, (c // 4) % 4, c % 4
    xy = c % 16
    right, left, twin = f + 2, f - 2, f + 1 - 2 * k
    partner = (c + 16) % 32

    def at_y(d):
        return c - y + (y + d) % 4

    def at_x(d):
        return c + 4 * ((x + d) % 4 - x)

    barrier = pltpu.get_barrier_semaphore()

    def greet(**where):
        pl.semaphore_signal(barrier, inc=1, device_id=where, device_id_type=pl.DeviceIdType.MESH)

    @pl.when(z < 3)
    def _():
        greet(fsdp=right)

    @pl.when(z > 0)
    def _():
        greet(fsdp=left)

    greet(fsdp=twin)
    for d in (1, 2, 3):
        greet(ctx=at_y(d))
    for d in (1, 2, 3):
        greet(ctx=at_x(d))
    greet(ctx=partner)

    @pl.when(c < 31)
    def _():
        greet(ctx=c + 1)

    @pl.when(c > 0)
    def _():
        greet(ctx=c - 1)

    own_g = pltpu.make_async_copy(g_ref, gbuf.at[f], l_sem.at[0])
    own_kv = pltpu.make_async_copy(kv_hbm, kv, l_sem.at[1])
    own_gate = pltpu.make_async_copy(gate_hbm, gate, l_sem.at[2])
    own_kv.start()
    own_g.start()
    own_gate.start()
    wbuf[xy, zh] = w_ref[...].astype(F32).T.astype(BF)
    taps[xy, zh] = filt_ref[...]
    own_kv.wait()
    tail[...] = kv[:, 896:]

    @pl.when(c == 0)
    def _():
        before[...] = jnp.zeros_like(before)

    @pl.when(c == 31)
    def _():
        after[...] = jnp.zeros_like(after)

    count = jnp.where(z < 3, 1, 0) + jnp.where(z > 0, 1, 0) + jnp.where(c < 31, 1, 0) + jnp.where(c > 0, 1, 0) + 8
    pl.semaphore_wait(barrier, count)
    own_g.wait()

    span = 512 // NCH

    def g_copy(p, ch, way):
        block = gbuf.at[2 * p + k, pl.ds(ch * span, span)]
        to = right if way == 0 else left
        return remote(block, block, g_send.at[p, ch, way], g_recv.at[p, ch], fsdp=to)

    def twin_copy(p, ch):
        block = gbuf.at[2 * p + k, pl.ds(ch * span, span)]
        return remote(block, block, s_send.at[p, ch], s_recv.at[p, ch], fsdp=twin)

    def wz_copy():
        block = wbuf.at[xy, zh]
        return remote(block, block, w_send.at[0], w_recv.at[0], ctx=partner)

    def wy_copy(d):
        block = wbuf.at[xy]
        return remote(block, block, w_send.at[d], w_recv.at[d], ctx=at_y(d))

    def wx_copy(d):
        block = wbuf.at[pl.ds(4 * x, 4)]
        return remote(block, block, w_send.at[4 + d], w_recv.at[4 + d], ctx=at_x(d))

    def wf_copy(d):
        block = wbuf.at[pl.ds(4 * ((x - d) % 4) + (0 if d == 1 else 2), 2)]
        return remote(block, block, w_send.at[8 + d], w_recv.at[8 + d], ctx=at_x(d))

    def b_copy():
        return remote(tail, before, b_send, b_recv, ctx=c + 1)

    def tz_copy():
        block = taps.at[xy, zh]
        return remote(block, block, t_send.at[0], t_recv.at[0], ctx=partner)

    def ty_copy(d):
        block = taps.at[xy]
        return remote(block, block, t_send.at[d], t_recv.at[d], ctx=at_y(d))

    def tx_copy(d):
        block = taps.at[pl.ds(4 * x, 4)]
        return remote(block, block, t_send.at[4 + d], t_recv.at[4 + d], ctx=at_x(d))

    tz_copy().start()

    @pl.when(c < 31)
    def _():
        b_copy().start()

    wz_copy().start()
    for ch in range(NCH):
        @pl.when(z < 3)
        def _():
            g_copy(z, ch, 0).start()

        @pl.when(z > 0)
        def _():
            g_copy(z, ch, 1).start()

        twin_copy(z, ch).start()

    mix[...] = jnp.zeros_like(mix)

    tz_copy().wait_recv()
    for d in (1, 3, 2):
        ty_copy(d).start()
    for d in (1, 3, 2):
        ty_copy(d).wait_recv()
    for d in (1, 3, 2):
        tx_copy(d).start()
    wz_copy().wait_recv()
    for d in (1, 3, 2):
        wy_copy(d).start()
    for d in (1, 3, 2):
        tx_copy(d).wait_recv()

    @pl.when(c > 0)
    def _():
        b_copy_in = b_copy()
        b_copy_in.wait_recv()

    own_gate.wait()

    def filter_forward(g, carry):
        rows = pl.ds(pl.multiple_of(g * 16, 16), 16)
        xs = [before[rows, :]] + [kv[rows, b * 128 : (b + 1) * 128] for b in range(8)]
        lhs = jnp.concatenate([jnp.concatenate([xs[b], xs[b + 1]], axis=1) for b in range(8)], axis=0)
        outs = conv_group(taps[g % 16, g // 16].astype(F32), lhs, False)
        for b in range(8):
            cols = slice(b * 128, (b + 1) * 128)
            narrow = outs[b].astype(BF)
            mixed[rows, cols] = narrow
            work[rows, cols] = (gate[rows, cols].astype(F32) * narrow.astype(F32)).astype(BF)
        return carry

    lax.fori_loop(0, 16, filter_forward, 0)
    for d in (1, 3, 2):
        wy_copy(d).wait_recv()
    for d in (1, 3):
        wx_copy(d).start()
    lax.fori_loop(16, 32, filter_forward, 0)

    def turn(i, carry):
        cols = pl.ds(pl.multiple_of(i * 128, 128), 128)
        gated_t[:, cols] = work[cols, :].astype(F32).T.astype(BF)
        return carry

    lax.fori_loop(0, 4, turn, 0)

    def y1_copy(b, j):
        return remote(y1s.at[b, j], y1b.at[b, j], y1_send.at[b, j], y1_recv.at[b, j], ctx=at_y(1 if j == 0 else 3))

    def y2_copy(b, j):
        return remote(y2s.at[b, j], y2b.at[b, j], y2_send.at[b, j], y2_recv.at[b, j], ctx=at_y(1 if j == 0 else 3))

    def x1_copy(b, j):
        return remote(x1s.at[b, j], x1b.at[b, j], x1_send.at[b, j], x1_recv.at[b, j], ctx=at_x(1 if j == 0 else 3))

    def x2_copy(b, j):
        return remote(x2s.at[b], x2b.at[b, j], x2_send.at[b], x2_recv.at[b, j], ctx=at_x(1 if j == 0 else 3))

    def z_copy():
        return remote(zs, zb, z_send, z_recv, ctx=partner)

    def multiply_rows(p):
        def tile(i, carry):
            b, h = 2 * p + i // 2, i % 2
            lhs = gbuf[b, pl.ds(pl.multiple_of(h * 256, 256), 256), :]
            part = jnp.dot(lhs, gated_t[...], preferred_element_type=F32)
            prod[b, pl.ds(2 * h, 2)] = part.reshape(2, 128, 512)
            return carry

        lax.fori_loop(0, 4, tile, 0)
        for i in range(2):
            b = 2 * p + i
            far = prod[b, (y + 2) % 4].astype(BF)
            y1s[b, 0] = far[:, :256]
            y1s[b, 1] = far[:, 256:]
            for j in range(2):
                y1_copy(b, j).start()

    def multiply_columns(p):
        def tile(i, carry):
            b, h, n = 2 * p + i // 4, (i // 2) % 2, i % 2
            rows = pl.ds(pl.multiple_of(h * 256, 256), 256)
            cols = pl.ds(pl.multiple_of(n * 512, 512), 512)
            lhs = jnp.concatenate([wbuf[4 * (b % 4) + q, b // 4, rows, :] for q in range(4)], axis=1)
            mix[rows, cols] += jnp.dot(lhs, gbuf[b, :, cols], preferred_element_type=F32)
            return carry

        lax.fori_loop(0, 8, tile, 0)

    def round_y2(p):
        for i in range(2):
            b = 2 * p + i
            y1_copy(b, 0).wait_recv()
            up = prod[b, (y + 1) % 4]
            y2s[b, 0, :, :256] = (up[:, :256] + y1b[b, 0].astype(F32)).astype(BF)
            y2s[b, 0, :, 256:] = up[:, 256:].astype(BF)
            y2_copy(b, 0).start()
            y1_copy(b, 1).wait_recv()
            down = prod[b, (y + 3) % 4]
            y2s[b, 1, :, :256] = down[:, :256].astype(BF)
            y2s[b, 1, :, 256:] = (down[:, 256:] + y1b[b, 1].astype(F32)).astype(BF)
            y2_copy(b, 1).start()

    def round_x1(p):
        for i in range(2):
            b = 2 * p + i
            y2_copy(b, 0).wait_recv()
            y2_copy(b, 1).wait_recv()
            total = prod[b, y] + y2b[b, 0].astype(F32) + y2b[b, 1].astype(F32)
            prod[b, y] = total

            @pl.when((x - b) % 4 == 2)
            def _():
                x1s[b, 0] = total[:, :256].astype(BF)
                x1s[b, 1] = total[:, 256:].astype(BF)
                for j in range(2):
                    x1_copy(b, j).start()

    def round_x2(p):
        for i in range(2):
            b = 2 * p + i
            role = (x - b) % 4

            @pl.when(role == 3)
            def _():
                x1_copy(b, 0).wait_recv()
                x2s[b, :, :256] = (prod[b, y, :, :256] + x1b[b, 0].astype(F32)).astype(BF)
                x2s[b, :, 256:] = prod[b, y, :, 256:].astype(BF)
                x2_copy(b, 0).start()

            @pl.when(role == 1)
            def _():
                x1_copy(b, 1).wait_recv()
                x2s[b, :, :256] = prod[b, y, :, :256].astype(BF)
                x2s[b, :, 256:] = (prod[b, y, :, 256:] + x1b[b, 1].astype(F32)).astype(BF)
                x2_copy(b, 1).start()

    def round_z(p):
        for i in range(2):
            b = 2 * p + i

            @pl.when((x - b) % 4 == 0)
            def _():
                x2_copy(b, 0).wait_recv()
                x2_copy(b, 1).wait_recv()
                total = prod[b, y] + x2b[b, 0].astype(F32) + x2b[b, 1].astype(F32)

                @pl.when(b // 4 == zh)
                def _():
                    prod[b, y] = total

                @pl.when(b // 4 != zh)
                def _():
                    zs[...] = total.astype(BF)
                    z_copy().start()

    def sides(s, act):
        @pl.when(z >= s)
        def _():
            act(z - s)

        @pl.when((s > 0) & (z + s < 4))
        def _():
            act(z + s)

    def step(s, carry):
        for ch in range(NCH):
            @pl.when((s > 0) & (z >= s))
            def _():
                g_copy(z - s, ch, 0).wait_recv()

                @pl.when(z < 3)
                def _():
                    g_copy(z - s, ch, 0).start()

                twin_copy(z - s, ch).start()

            @pl.when((s > 0) & (z + s < 4))
            def _():
                g_copy(z + s, ch, 1).wait_recv()

                @pl.when(z > 0)
                def _():
                    g_copy(z + s, ch, 1).start()

                twin_copy(z + s, ch).start()

        def arrive(p):
            for ch in range(NCH):
                twin_copy(p, ch).wait_recv()
            multiply_rows(p)

        sides(s, arrive)

        @pl.when(s > 0)
        def _():
            sides(s - 1, round_x2)

        @pl.when(s == 1)
        def _():
            wx_copy(1).wait_recv()
            wf_copy(1).start()
            wx_copy(3).wait_recv()
            wf_copy(3).start()

        @pl.when(s == 2)
        def _():
            wf_copy(1).wait_recv()
            wf_copy(3).wait_recv()

        @pl.when(s >= 2)
        def _():
            def late(q, carry):
                sides(q, multiply_columns)
                return carry

            lax.fori_loop(jnp.where(s == 2, 0, 3), s + 1, late, 0)

        sides(s, round_y2)

        @pl.when(s > 0)
        def _():
            sides(s - 1, round_z)

        sides(s, round_x1)
        return carry

    lax.fori_loop(0, 4, step, 0)

    def h_copy():
        return remote(head, after, h_send, h_recv, ctx=c - 1)

    def finish_head(i, carry):
        rows = pl.ds(pl.multiple_of(i * 64, 64), 64)
        head[rows, :] = (mix[rows, :128] * gate[rows, :128].astype(F32)).astype(BF)
        return carry

    lax.fori_loop(0, 8, finish_head, 0)

    @pl.when(c > 0)
    def _():
        h_copy().start()

    def finish(i, carry):
        rows = pl.ds(pl.multiple_of(i * 32, 32), 32)
        wide = mix[rows, :]
        work[rows, :] = (wide * gate[rows, :].astype(F32)).astype(BF)
        mix[rows, :] = wide * mixed[rows, :].astype(F32)
        return carry

    lax.fori_loop(0, 16, finish, 0)
    out_gate = pltpu.make_async_copy(mix, gate_grad_ref, l_sem.at[3])
    out_gate.start()
    sides(3, round_x2)

    @pl.when(c < 31)
    def _():
        h_copy().wait_recv()

    def fy_copy(d):
        return remote(fsum.at[(y + d) % 4], fy.at[d - 1], f_send.at[d], f_recv.at[d], ctx=at_y(d))

    def fx_copy(d):
        return remote(fxs.at[(x + d) % 4], fx.at[d - 1], f_send.at[4 + d], f_recv.at[4 + d], ctx=at_x(d))

    def fz_copy():
        return remote(fzs, fz, f_send.at[0], f_recv.at[0], ctx=partner)

    for d in (2, 1, 3, 0):
        def filter_back(i, carry):
            g = 4 * i + (y + d) % 4
            rows = pl.ds(pl.multiple_of(g * 16, 16), 16)
            kv_grads, taps_part = back_group(
                before, kv, work, after, rows, taps[g % 16, g // 16].astype(F32), part
            )
            for b in range(8):
                kv_grad_ref[rows, b * 128 : (b + 1) * 128] = kv_grads[b].astype(BF)
            fsum[(y + d) % 4, i % 4, i // 4] = taps_part
            return carry

        lax.fori_loop(0, 8, filter_back, 0)
        if d:
            fy_copy(d).start()
        if d == 2:
            sides(3, round_z)

    for d in (2, 1, 3):
        fy_copy(d).wait_recv()
    fxs[...] = fsum[y] + fy[0] + fy[1] + fy[2]
    for d in (2, 1, 3):
        fx_copy(d).start()
    z_copy().wait_recv()
    w_grad_ref[...] = (prod[4 * zh + x, y] + zb[...].astype(F32)) * scale
    for d in (2, 1, 3):
        fx_copy(d).wait_recv()
    fzs[...] = fxs[x, 1 - zh] + fx[0, 1 - zh] + fx[1, 1 - zh] + fx[2, 1 - zh]
    fz_copy().start()
    mine = fxs[x, zh] + fx[0, zh] + fx[1, zh] + fx[2, zh]
    fz_copy().wait_recv()
    filt_grad_ref[...] = (mine + fz[...]) * scale
    out_gate.wait()

    def sent_blocks(p, carry):
        for ch in range(NCH):
            @pl.when((p <= z) & (z < 3))
            def _():
                g_copy(p, ch, 0).wait_send()

            @pl.when((p >= z) & (z > 0))
            def _():
                g_copy(p, ch, 1).wait_send()

            twin_copy(p, ch).wait_send()
        return carry

    lax.fori_loop(0, 4, sent_blocks, 0)

    def sent_sums(b, carry):
        for j in range(2):
            y1_copy(b, j).wait_send()
            y2_copy(b, j).wait_send()
        role = (x - b) % 4

        @pl.when(role == 2)
        def _():
            for j in range(2):
                x1_copy(b, j).wait_send()

        @pl.when(role % 2 == 1)
        def _():
            x2_copy(b, 0).wait_send()

        return carry

    lax.fori_loop(0, 8, sent_sums, 0)
    z_copy().wait_send()
    wz_copy().wait_send()
    for d in (1, 2, 3):
        wy_copy(d).wait_send()
    for d in (1, 3):
        wx_copy(d).wait_send()
        wf_copy(d).wait_send()

    @pl.when(c > 0)
    def _():
        h_copy().wait_send()

    @pl.when(c < 31)
    def _():
        b_copy().wait_send()

    tz_copy().wait_send()
    fz_copy().wait_send()
    for d in (1, 2, 3):
        ty_copy(d).wait_send()
        tx_copy(d).wait_send()
        fy_copy(d).wait_send()
        fx_copy(d).wait_send()


def exchange(out_grad, w_out, gate, kv, filters, scale):
    vmem = pl.BlockSpec(memory_space=pltpu.VMEM)
    hbm = pl.BlockSpec(memory_space=pl.ANY)
    dma = pltpu.SemaphoreType.DMA
    return pl.pallas_call(
        functools.partial(exchange_kernel, scale=scale),
        out_shape=[
            jax.ShapeDtypeStruct((512, 1024), F32),
            jax.ShapeDtypeStruct((512, 1024), BF),
            jax.ShapeDtypeStruct((16, 128), F32),
            jax.ShapeDtypeStruct((128, 512), F32),
        ],
        in_specs=[hbm, vmem, hbm, hbm, vmem],
        out_specs=[hbm, vmem, vmem, vmem],
        scratch_shapes=[
            pltpu.VMEM((8, 512, 1024), BF),
            pltpu.VMEM((16, 2, 512, 128), BF),
            pltpu.VMEM((1024, 512), BF),
            pltpu.VMEM((8, 4, 128, 512), F32),
            pltpu.VMEM((512, 1024), F32),
            pltpu.VMEM((512, 128), BF),
            pltpu.VMEM((512, 128), BF),
            pltpu.VMEM((512, 128), BF),
            pltpu.VMEM((512, 128), BF),
            pltpu.VMEM((16, 2, 16, 128), BF),
            pltpu.VMEM((512, 1024), BF),
            pltpu.VMEM((512, 1024), BF),
            pltpu.VMEM((512, 1024), BF),
            pltpu.VMEM((512, 1024), BF),
            pltpu.VMEM((16, 8, 128), F32),
            pltpu.VMEM((4, 4, 2, 16, 128), F32),
            pltpu.VMEM((3, 4, 2, 16, 128), F32),
            pltpu.VMEM((3, 2, 16, 128), F32),
            pltpu.VMEM((16, 128), F32),
            pltpu.VMEM((4, 2, 16, 128), F32),
            pltpu.VMEM((16, 128), F32),
            pltpu.VMEM((8, 2, 128, 256), BF),
            pltpu.VMEM((8, 2, 128, 256), BF),
            pltpu.VMEM((8, 2, 128, 512), BF),
            pltpu.VMEM((8, 2, 128, 512), BF),
            pltpu.VMEM((8, 2, 128, 256), BF),
            pltpu.VMEM((8, 2, 128, 256), BF),
            pltpu.VMEM((8, 128, 512), BF),
            pltpu.VMEM((8, 2, 128, 512), BF),
            pltpu.VMEM((128, 512), BF),
            pltpu.VMEM((128, 512), BF),
            dma((4, NCH, 2)), dma((4, NCH)), dma((4, NCH)), dma((4, NCH)), dma((12,)), dma((12,)),
            dma((8, 2)), dma((8, 2)), dma((8, 2)), dma((8, 2)), dma((8, 2)), dma((8, 2)), dma((8,)), dma((8, 2)),
            dma, dma, dma, dma, dma, dma, dma((8,)), dma((8,)), dma((8,)), dma((8,)), dma((4,)),
        ],
        compiler_params=pltpu.CompilerParams(
            collective_id=0, has_side_effects=True, vmem_limit_bytes=60 << 20
        ),
    )(out_grad, w_out, gate, kv, filters)


def on_device(out_grad, gate_values, kv_product, w_out, filters):
    scale = 1.0 / math.sqrt(lax.axis_size("ctx") * out_grad.shape[1])
    gate_grad, kv_grad, filter_grad, w_grad = exchange(
        out_grad, w_out, gate_values, kv_product, filters.reshape(filters.shape[2:]), scale
    )
    return (gate_grad, kv_grad, filter_grad.reshape(filters.shape), w_grad)


def solution(mesh):
    in_specs = (
        P("fsdp", "ctx"),
        P("fsdp", "ctx"),
        P("fsdp", "ctx"),
        P("ctx", "fsdp"),
        P("fsdp", "ctx", None, None),
    )
    out_specs = (P("fsdp", "ctx"), P("fsdp", "ctx"), P("fsdp", "ctx", None, None), P("ctx", "fsdp"))
    return jax.shard_map(
        on_device, mesh=mesh, in_specs=in_specs, out_specs=out_specs, check_vma=False
    )
```

```python
import functools
import math

import jax
import jax.numpy as jnp
from jax import lax
from jax.experimental import pallas as pl
from jax.experimental.pallas import tpu as pltpu
from jax.sharding import PartitionSpec as P

F32 = jnp.float32
BF = jnp.bfloat16


def bands(row):
    rows = lax.broadcasted_iota(jnp.int32, (128, 128), 0)
    lanes = lax.broadcasted_iota(jnp.int32, (128, 128), 1)
    turned = pltpu.roll(jnp.broadcast_to(row, (128, 128)), 0, 1, stride=1, stride_axis=0)
    near = jnp.where(lanes >= rows, turned, 0.0).astype(BF)
    far = jnp.where(lanes < rows, turned, 0.0).astype(BF)
    return far, near


def stack_blocks(parts):
    return jnp.concatenate(
        [jnp.concatenate([parts[b], parts[b + 1]], axis=1) for b in range(8)], axis=0
    )


def keep_own(out, product, ch, column):
    sub = lax.broadcasted_iota(jnp.int32, (8, 128), 0)
    half = ch // 8
    for b in range(8):
        start = b * 16 + half * 8
        piece = product[start : start + 8, column * 128 : (column + 1) * 128]
        old = out[b][half]
        out[b][half] = piece if old is None else jnp.where(sub == ch % 8, piece, old)


def conv_group(taps, lhs, _):
    out = [[None, None] for _ in range(8)]
    for pair in range(8):
        cols = [jnp.concatenate(bands(taps[ch : ch + 1, :]), axis=0) for ch in (2 * pair, 2 * pair + 1)]
        product = jnp.dot(lhs, jnp.concatenate(cols, axis=1), preferred_element_type=F32)
        for i in range(2):
            keep_own(out, product, 2 * pair + i, i)
    return [jnp.concatenate(o, axis=0) for o in out]


def back_group(before, kv, grad, after, rows, taps, part):
    xs = [before[rows, :]] + [kv[rows, b * 128 : (b + 1) * 128] for b in range(8)]
    gs = [grad[rows, b * 128 : (b + 1) * 128] for b in range(8)] + [after[rows, :]]
    row_at = lax.broadcasted_iota(jnp.int32, (128, 128), 0)
    lane_at = lax.broadcasted_iota(jnp.int32, (128, 128), 1)
    lhs = stack_blocks(gs)
    x_turned = stack_blocks(xs).astype(F32).T.astype(BF)
    wide = jnp.concatenate(gs[:8], axis=0).astype(F32)
    out = [[None, None] for _ in range(8)]
    for pair in range(8):
        band_rows, own_grad = [], []
        for ch in (2 * pair, 2 * pair + 1):
            far, near = bands(taps[ch : ch + 1, :])
            band_rows.append(jnp.concatenate([near, far], axis=1))
            own_grad.append(jnp.where(row_at % 16 == ch, wide, 0.0).astype(BF))
        product = lax.dot_general(
            lhs, jnp.concatenate(band_rows, axis=0), (((1,), (1,)), ((), ())), preferred_element_type=F32
        )
        outer = jnp.dot(x_turned, jnp.concatenate(own_grad, axis=1), preferred_element_type=F32)
        for i in range(2):
            ch = 2 * pair + i
            keep_own(out, product, ch, i)
            cols = slice(i * 128, (i + 1) * 128)
            both = jnp.where(lane_at >= row_at, outer[128:, cols], outer[:128, cols])
            acc = both[0:8]
            for v in range(1, 16):
                acc = acc + pltpu.roll(both[8 * v : 8 * v + 8], 128 - 8 * v, 1)
            part[ch] = acc
    taps_part = part[:, 0, :]
    for u in range(1, 8):
        taps_part = taps_part + pltpu.roll(part[:, u, :], 128 - u, 1)
    return [jnp.concatenate(o, axis=0) for o in out], taps_part


NCH = 2


def remote(src, dst, send, recv, **where):
    return pltpu.make_async_remote_copy(src, dst, send, recv, device_id=where, device_id_type=pl.DeviceIdType.MESH)


def exchange_kernel(
    g_ref, w_ref, gate_hbm, kv_hbm, filt_ref,
    gate_grad_ref, kv_grad_ref, filt_grad_ref, w_grad_ref,
    gbuf, wbuf, gated_t, prod, mix, head, after, tail, before, taps,
    gate, kv, mixed, work, part, fsum, fin,
    y1s, y1b, y2s, y2b, x1s, x1b, x2s, x2b, zs, zb,
    g_send, g_recv, s_send, s_recv, w_send, w_recv,
    y1_send, y1_recv, y2_send, y2_recv, x1_send, x1_recv, x2_send, x2_recv, z_send, z_recv,
    h_send, h_recv, b_send, b_recv, t_send, t_recv, f_send, f_recv, l_sem, *, scale,
):
    c = lax.axis_index("ctx")
    f = lax.axis_index("fsdp")
    z, k = f // 2, f % 2
    zh, x, y = c // 16, (c // 4) % 4, c % 4
    xy = c % 16
    right, left, twin = f + 2, f - 2, f + 1 - 2 * k
    partner = (c + 16) % 32

    def at_y(d):
        return c - y + (y + d) % 4

    def at_x(d):
        return c + 4 * ((x + d) % 4 - x)

    barrier = pltpu.get_barrier_semaphore()

    def greet(**where):
        pl.semaphore_signal(barrier, inc=1, device_id=where, device_id_type=pl.DeviceIdType.MESH)

    @pl.when(z < 3)
    def _():
        greet(fsdp=right)

    @pl.when(z > 0)
    def _():
        greet(fsdp=left)

    greet(fsdp=twin)

    def greet_peer(i, carry):
        greet(ctx=(c + i) % 32)
        return carry

    lax.fori_loop(1, 32, greet_peer, 0)
    own_g = pltpu.make_async_copy(g_ref, gbuf.at[f], l_sem.at[0])
    own_kv = pltpu.make_async_copy(kv_hbm, kv, l_sem.at[1])
    own_gate = pltpu.make_async_copy(gate_hbm, gate, l_sem.at[2])
    own_kv.start()
    own_g.start()
    own_gate.start()
    wbuf[xy, zh] = w_ref[...].astype(F32).T.astype(BF)
    taps[xy, zh] = filt_ref[...]
    own_kv.wait()
    tail[...] = kv[:, 896:]

    @pl.when(c == 0)
    def _():
        before[...] = jnp.zeros_like(before)

    @pl.when(c == 31)
    def _():
        after[...] = jnp.zeros_like(after)

    count = jnp.where(z < 3, 1, 0) + jnp.where(z > 0, 1, 0) + 32
    pl.semaphore_wait(barrier, count)
    own_g.wait()

    span = 512 // NCH

    def g_copy(p, ch, way):
        block = gbuf.at[2 * p + k, pl.ds(ch * span, span)]
        return remote(block, block, g_send.at[p, ch, way], g_recv.at[p, ch], fsdp=right - 4 * way)

    def twin_copy(p, ch):
        block = gbuf.at[2 * p + k, pl.ds(ch * span, span)]
        return remote(block, block, s_send.at[p, ch], s_recv.at[p, ch], fsdp=twin)

    def wz_copy():
        block = wbuf.at[xy, zh]
        return remote(block, block, w_send.at[0], w_recv.at[0], ctx=partner)

    def wy_copy(d):
        block = wbuf.at[xy]
        return remote(block, block, w_send.at[d], w_recv.at[d], ctx=at_y(d))

    def wx_copy(d):
        block = wbuf.at[pl.ds(4 * x, 4)]
        return remote(block, block, w_send.at[4 + d], w_recv.at[4 + d], ctx=at_x(d))

    def wf_copy(d):
        block = wbuf.at[pl.ds(4 * ((x - d) % 4) + (0 if d == 1 else 2), 2)]
        return remote(block, block, w_send.at[8 + d], w_recv.at[8 + d], ctx=at_x(d))

    def b_copy():
        return remote(tail, before, b_send, b_recv, ctx=c + 1)

    def t_copy(i):
        block = taps.at[xy, zh]
        return remote(block, block, t_send.at[i], t_recv.at[i], ctx=(c + i) % 32)

    def send_taps(i, carry):
        t_copy(i).start()
        return carry

    lax.fori_loop(1, 32, send_taps, 0)

    @pl.when(c < 31)
    def _():
        b_copy().start()

    wz_copy().start()
    for ch in range(NCH):
        @pl.when(z < 3)
        def _():
            g_copy(z, ch, 0).start()

        @pl.when(z > 0)
        def _():
            g_copy(z, ch, 1).start()

        twin_copy(z, ch).start()

    mix[...] = jnp.zeros_like(mix)

    def have_taps(i, carry):
        t_copy(i).wait_recv()
        return carry

    lax.fori_loop(1, 32, have_taps, 0)
    wz_copy().wait_recv()
    for d in (1, 3, 2):
        wy_copy(d).start()

    @pl.when(c > 0)
    def _():
        b_copy().wait_recv()

    own_gate.wait()

    def filter_forward(g, carry):
        rows = pl.ds(pl.multiple_of(g * 16, 16), 16)
        xs = [before[rows, :]] + [kv[rows, b * 128 : (b + 1) * 128] for b in range(8)]
        lhs = jnp.concatenate([jnp.concatenate([xs[b], xs[b + 1]], axis=1) for b in range(8)], axis=0)
        outs = conv_group(taps[g % 16, g // 16].astype(F32), lhs, False)
        for b in range(8):
            cols = slice(b * 128, (b + 1) * 128)
            narrow = outs[b].astype(BF)
            mixed[rows, cols] = narrow
            work[rows, cols] = (gate[rows, cols].astype(F32) * narrow.astype(F32)).astype(BF)
        return carry

    def sides(s, act):
        if s == 0:
            act(z)
            return

        def one(side, carry):
            p = z - s + 2 * s * side

            @pl.when((p >= 0) & (p < 4))
            def _():
                act(p)

            return carry

        lax.fori_loop(0, 2, one, 0)

    def pass_on(s, ch):
        def act(p):
            g_copy(p, ch, 0).wait_recv()

            @pl.when((p < z) & (z < 3))
            def _():
                g_copy(p, ch, 0).start()

            @pl.when((p > z) & (z > 0))
            def _():
                g_copy(p, ch, 1).start()

            twin_copy(p, ch).start()

        sides(s, act)

    lax.fori_loop(0, 16, filter_forward, 0)
    for d in (1, 3, 2):
        wy_copy(d).wait_recv()
    for d in (1, 3):
        wx_copy(d).start()
    pass_on(1, 0)
    lax.fori_loop(16, 32, filter_forward, 0)

    def turn(i, carry):
        cols = pl.ds(pl.multiple_of(i * 128, 128), 128)
        gated_t[:, cols] = work[cols, :].astype(F32).T.astype(BF)
        return carry

    lax.fori_loop(0, 4, turn, 0)

    def y1_copy(b, j):
        return remote(y1s.at[b, j], y1b.at[b, j], y1_send.at[b, j], y1_recv.at[b, j], ctx=at_y(1 if j == 0 else 3))

    def y2_copy(b, j):
        return remote(y2s.at[b, j], y2b.at[b, j], y2_send.at[b, j], y2_recv.at[b, j], ctx=at_y(1 if j == 0 else 3))

    def x1_copy(b, j):
        return remote(x1s.at[b, j], x1b.at[b, j], x1_send.at[b, j], x1_recv.at[b, j], ctx=at_x(1 if j == 0 else 3))

    def x2_copy(b, j):
        return remote(x2s.at[b], x2b.at[b, j], x2_send.at[b], x2_recv.at[b, j], ctx=at_x(1 if j == 0 else 3))

    def z_copy():
        return remote(zs, zb, z_send, z_recv, ctx=partner)

    def multiply_rows(p):
        def tile(i, carry):
            b, h = 2 * p + i // 2, i % 2
            lhs = gbuf[b, pl.ds(pl.multiple_of(h * 256, 256), 256), :]
            part = jnp.dot(lhs, gated_t[...], preferred_element_type=F32)
            prod[b, pl.ds(2 * h, 2)] = part.reshape(2, 128, 512)
            return carry

        lax.fori_loop(0, 4, tile, 0)
        for i in range(2):
            b = 2 * p + i
            far = prod[b, (y + 2) % 4].astype(BF)
            y1s[b, 0] = far[:, :256]
            y1s[b, 1] = far[:, 256:]
            for j in range(2):
                y1_copy(b, j).start()

    def multiply_columns(p):
        def tile(i, carry):
            b, h, n = 2 * p + i // 4, (i // 2) % 2, i % 2
            rows = pl.ds(pl.multiple_of(h * 256, 256), 256)
            cols = pl.ds(pl.multiple_of(n * 512, 512), 512)
            lhs = jnp.concatenate([wbuf[4 * (b % 4) + q, b // 4, rows, :] for q in range(4)], axis=1)
            mix[rows, cols] += jnp.dot(lhs, gbuf[b, :, cols], preferred_element_type=F32)
            return carry

        lax.fori_loop(0, 8, tile, 0)

    def round_y2(p):
        for i in range(2):
            b = 2 * p + i
            y1_copy(b, 0).wait_recv()
            up = prod[b, (y + 1) % 4]
            y2s[b, 0, :, :256] = (up[:, :256] + y1b[b, 0].astype(F32)).astype(BF)
            y2s[b, 0, :, 256:] = up[:, 256:].astype(BF)
            y2_copy(b, 0).start()
            y1_copy(b, 1).wait_recv()
            down = prod[b, (y + 3) % 4]
            y2s[b, 1, :, :256] = down[:, :256].astype(BF)
            y2s[b, 1, :, 256:] = (down[:, 256:] + y1b[b, 1].astype(F32)).astype(BF)
            y2_copy(b, 1).start()

    def round_x1(p):
        for i in range(2):
            b = 2 * p + i
            y2_copy(b, 0).wait_recv()
            y2_copy(b, 1).wait_recv()
            total = prod[b, y] + y2b[b, 0].astype(F32) + y2b[b, 1].astype(F32)
            prod[b, y] = total

            @pl.when((x - b) % 4 == 2)
            def _():
                x1s[b, 0] = total[:, :256].astype(BF)
                x1s[b, 1] = total[:, 256:].astype(BF)
                for j in range(2):
                    x1_copy(b, j).start()

    def round_x2(p):
        for i in range(2):
            b = 2 * p + i
            role = (x - b) % 4

            @pl.when(role == 3)
            def _():
                x1_copy(b, 0).wait_recv()
                x2s[b, :, :256] = (prod[b, y, :, :256] + x1b[b, 0].astype(F32)).astype(BF)
                x2s[b, :, 256:] = prod[b, y, :, 256:].astype(BF)
                x2_copy(b, 0).start()

            @pl.when(role == 1)
            def _():
                x1_copy(b, 1).wait_recv()
                x2s[b, :, :256] = prod[b, y, :, :256].astype(BF)
                x2s[b, :, 256:] = (prod[b, y, :, 256:] + x1b[b, 1].astype(F32)).astype(BF)
                x2_copy(b, 1).start()

    def round_z(p):
        for i in range(2):
            b = 2 * p + i

            @pl.when((x - b) % 4 == 0)
            def _():
                x2_copy(b, 0).wait_recv()
                x2_copy(b, 1).wait_recv()
                total = prod[b, y] + x2b[b, 0].astype(F32) + x2b[b, 1].astype(F32)

                @pl.when(b // 4 == zh)
                def _():
                    prod[b, y] = total

                @pl.when(b // 4 != zh)
                def _():
                    zs[...] = total.astype(BF)
                    z_copy().start()

    def arrive(p):
        for ch in range(NCH):
            twin_copy(p, ch).wait_recv()
        multiply_rows(p)

    arrive(z)
    sides(0, round_y2)
    pass_on(1, 1)
    sides(1, arrive)
    sides(0, round_x1)
    pass_on(2, 0)
    sides(1, round_y2)
    sides(0, round_x2)
    wx_copy(1).wait_recv()
    wf_copy(1).start()
    wx_copy(3).wait_recv()
    wf_copy(3).start()
    pass_on(2, 1)
    sides(2, arrive)
    sides(1, round_x1)
    sides(0, round_z)
    pass_on(3, 0)
    sides(2, round_y2)
    sides(1, round_x2)
    wf_copy(1).wait_recv()
    wf_copy(3).wait_recv()
    for s in (0, 1, 2):
        sides(s, multiply_columns)
    pass_on(3, 1)
    sides(3, arrive)
    sides(2, round_x1)
    sides(1, round_z)
    sides(3, multiply_columns)

    def h_copy():
        return remote(head, after, h_send, h_recv, ctx=c - 1)

    def finish_head(i, carry):
        rows = pl.ds(pl.multiple_of(i * 64, 64), 64)
        head[rows, :] = (mix[rows, :128] * gate[rows, :128].astype(F32)).astype(BF)
        return carry

    lax.fori_loop(0, 8, finish_head, 0)

    @pl.when(c > 0)
    def _():
        h_copy().start()

    def finish(i, carry):
        rows = pl.ds(pl.multiple_of(i * 32, 32), 32)
        wide = mix[rows, :]
        work[rows, :] = (wide * gate[rows, :].astype(F32)).astype(BF)
        mix[rows, :] = wide * mixed[rows, :].astype(F32)
        return carry

    lax.fori_loop(0, 16, finish, 0)
    out_gate = pltpu.make_async_copy(mix, gate_grad_ref, l_sem.at[3])
    out_gate.start()
    sides(3, round_y2)
    sides(2, round_x2)

    @pl.when(c < 31)
    def _():
        h_copy().wait_recv()

    def f_copy(i):
        return remote(fsum.at[(c + i) % 32], fin.at[i], f_send.at[i], f_recv.at[i], ctx=(c + i) % 32)

    def filter_back(i, carry):
        g = (c + i) % 32
        rows = pl.ds(pl.multiple_of(g * 16, 16), 16)
        kv_grads, taps_part = back_group(
            before, kv, work, after, rows, taps[g % 16, g // 16].astype(F32), part
        )
        for b in range(8):
            kv_grad_ref[rows, b * 128 : (b + 1) * 128] = kv_grads[b].astype(BF)
        fsum[g] = taps_part

        @pl.when(i < 32)
        def _():
            f_copy(i).start()

        return carry

    lax.fori_loop(1, 9, filter_back, 0)
    sides(3, round_x1)
    lax.fori_loop(9, 17, filter_back, 0)
    sides(3, round_x2)
    sides(2, round_z)
    lax.fori_loop(17, 25, filter_back, 0)
    sides(3, round_z)
    lax.fori_loop(25, 33, filter_back, 0)
    z_copy().wait_recv()
    w_grad_ref[...] = (prod[4 * zh + x, y] + zb[...].astype(F32)) * scale

    def gather_taps(i, total):
        f_copy(i).wait_recv()
        return total + fin[i]

    filt_grad_ref[...] = lax.fori_loop(1, 32, gather_taps, fsum[c]) * scale
    out_gate.wait()

    def sent_blocks(p, carry):
        for ch in range(NCH):
            @pl.when((p <= z) & (z < 3))
            def _():
                g_copy(p, ch, 0).wait_send()

            @pl.when((p >= z) & (z > 0))
            def _():
                g_copy(p, ch, 1).wait_send()

            twin_copy(p, ch).wait_send()
        return carry

    lax.fori_loop(0, 4, sent_blocks, 0)

    def sent_sums(b, carry):
        for j in range(2):
            y1_copy(b, j).wait_send()
            y2_copy(b, j).wait_send()
        role = (x - b) % 4

        @pl.when(role == 2)
        def _():
            for j in range(2):
                x1_copy(b, j).wait_send()

        @pl.when(role % 2 == 1)
        def _():
            x2_copy(b, 0).wait_send()

        return carry

    lax.fori_loop(0, 8, sent_sums, 0)
    z_copy().wait_send()
    wz_copy().wait_send()
    for d in (1, 2, 3):
        wy_copy(d).wait_send()
    for d in (1, 3):
        wx_copy(d).wait_send()
        wf_copy(d).wait_send()

    @pl.when(c > 0)
    def _():
        h_copy().wait_send()

    @pl.when(c < 31)
    def _():
        b_copy().wait_send()

    def sent_small(i, carry):
        t_copy(i).wait_send()
        f_copy(i).wait_send()
        return carry

    lax.fori_loop(1, 32, sent_small, 0)


def exchange(out_grad, w_out, gate, kv, filters, scale):
    vmem = pl.BlockSpec(memory_space=pltpu.VMEM)
    hbm = pl.BlockSpec(memory_space=pl.ANY)
    dma = pltpu.SemaphoreType.DMA
    return pl.pallas_call(
        functools.partial(exchange_kernel, scale=scale),
        out_shape=[
            jax.ShapeDtypeStruct((512, 1024), F32),
            jax.ShapeDtypeStruct((512, 1024), BF),
            jax.ShapeDtypeStruct((16, 128), F32),
            jax.ShapeDtypeStruct((128, 512), F32),
        ],
        in_specs=[hbm, vmem, hbm, hbm, vmem],
        out_specs=[hbm, vmem, vmem, vmem],
        scratch_shapes=[
            pltpu.VMEM((8, 512, 1024), BF),
            pltpu.VMEM((16, 2, 512, 128), BF),
            pltpu.VMEM((1024, 512), BF),
            pltpu.VMEM((8, 4, 128, 512), F32),
            pltpu.VMEM((512, 1024), F32),
            pltpu.VMEM((512, 128), BF),
            pltpu.VMEM((512, 128), BF),
            pltpu.VMEM((512, 128), BF),
            pltpu.VMEM((512, 128), BF),
            pltpu.VMEM((16, 2, 16, 128), BF),
            pltpu.VMEM((512, 1024), BF),
            pltpu.VMEM((512, 1024), BF),
            pltpu.VMEM((512, 1024), BF),
            pltpu.VMEM((512, 1024), BF),
            pltpu.VMEM((16, 8, 128), F32),
            pltpu.VMEM((32, 16, 128), F32),
            pltpu.VMEM((32, 16, 128), F32),
            pltpu.VMEM((8, 2, 128, 256), BF),
            pltpu.VMEM((8, 2, 128, 256), BF),
            pltpu.VMEM((8, 2, 128, 512), BF),
            pltpu.VMEM((8, 2, 128, 512), BF),
            pltpu.VMEM((8, 2, 128, 256), BF),
            pltpu.VMEM((8, 2, 128, 256), BF),
            pltpu.VMEM((8, 128, 512), BF),
            pltpu.VMEM((8, 2, 128, 512), BF),
            pltpu.VMEM((128, 512), BF),
            pltpu.VMEM((128, 512), BF),
            dma((4, NCH, 2)), dma((4, NCH)), dma((4, NCH)), dma((4, NCH)), dma((12,)), dma((12,)),
            dma((8, 2)), dma((8, 2)), dma((8, 2)), dma((8, 2)), dma((8, 2)), dma((8, 2)), dma((8,)), dma((8, 2)),
            dma, dma, dma, dma, dma, dma, dma((32,)), dma((32,)), dma((32,)), dma((32,)), dma((4,)),
        ],
        compiler_params=pltpu.CompilerParams(
            collective_id=0, has_side_effects=True, vmem_limit_bytes=60 << 20
        ),
    )(out_grad, w_out, gate, kv, filters)


def on_device(out_grad, gate_values, kv_product, w_out, filters):
    scale = 1.0 / math.sqrt(lax.axis_size("ctx") * out_grad.shape[1])
    gate_grad, kv_grad, filter_grad, w_grad = exchange(
        out_grad, w_out, gate_values, kv_product, filters.reshape(filters.shape[2:]), scale
    )
    return (gate_grad, kv_grad, filter_grad.reshape(filters.shape), w_grad)


def solution(mesh):
    in_specs = (
        P("fsdp", "ctx"),
        P("fsdp", "ctx"),
        P("fsdp", "ctx"),
        P("ctx", "fsdp"),
        P("fsdp", "ctx", None, None),
    )
    out_specs = (P("fsdp", "ctx"), P("fsdp", "ctx"), P("fsdp", "ctx", None, None), P("ctx", "fsdp"))
    return jax.shard_map(
        on_device, mesh=mesh, in_specs=in_specs, out_specs=out_specs, check_vma=False
    )
```

```python
import functools
import math

import jax
import jax.numpy as jnp
from jax import lax
from jax.experimental import pallas as pl
from jax.experimental.pallas import tpu as pltpu
from jax.sharding import PartitionSpec as P

F32 = jnp.float32
BF = jnp.bfloat16


def bands(row):
    rows = lax.broadcasted_iota(jnp.int32, (128, 128), 0)
    lanes = lax.broadcasted_iota(jnp.int32, (128, 128), 1)
    turned = pltpu.roll(jnp.broadcast_to(row, (128, 128)), 0, 1, stride=1, stride_axis=0)
    near = jnp.where(lanes >= rows, turned, 0.0).astype(BF)
    far = jnp.where(lanes < rows, turned, 0.0).astype(BF)
    return far, near


def stack_blocks(parts):
    return jnp.concatenate(
        [jnp.concatenate([parts[b], parts[b + 1]], axis=1) for b in range(8)], axis=0
    )


def keep_own(out, product, ch, column):
    sub = lax.broadcasted_iota(jnp.int32, (8, 128), 0)
    half = ch // 8
    for b in range(8):
        start = b * 16 + half * 8
        piece = product[start : start + 8, column * 128 : (column + 1) * 128]
        old = out[b][half]
        out[b][half] = piece if old is None else jnp.where(sub == ch % 8, piece, old)


def conv_group(taps, lhs, _):
    out = [[None, None] for _ in range(8)]
    for pair in range(8):
        cols = [jnp.concatenate(bands(taps[ch : ch + 1, :]), axis=0) for ch in (2 * pair, 2 * pair + 1)]
        product = jnp.dot(lhs, jnp.concatenate(cols, axis=1), preferred_element_type=F32)
        for i in range(2):
            keep_own(out, product, 2 * pair + i, i)
    return [jnp.concatenate(o, axis=0) for o in out]


def back_group(before, kv, grad, after, rows, taps, part, kv_grad, with_kv, with_taps):
    gs = [grad[rows, b * 128 : (b + 1) * 128] for b in range(8)]
    row_at = lax.broadcasted_iota(jnp.int32, (128, 128), 0)
    lane_at = lax.broadcasted_iota(jnp.int32, (128, 128), 1)
    if with_kv:
        lhs = stack_blocks(gs + [after[rows, :]])
    if with_taps:
        xs = [before[rows, :]] + [kv[rows, b * 128 : (b + 1) * 128] for b in range(8)]
        x_turned = stack_blocks(xs).astype(F32).T.astype(BF)
        wide = jnp.concatenate(gs, axis=0).astype(F32)
    out = [[None, None] for _ in range(8)]
    for pair in range(8):
        band_rows, own_grad = [], []
        for ch in (2 * pair, 2 * pair + 1):
            if with_kv:
                far, near = bands(taps[ch : ch + 1, :])
                band_rows.append(jnp.concatenate([near, far], axis=1))
            if with_taps:
                own_grad.append(jnp.where(row_at % 16 == ch, wide, 0.0).astype(BF))
        if with_kv:
            product = lax.dot_general(
                lhs, jnp.concatenate(band_rows, axis=0), (((1,), (1,)), ((), ())), preferred_element_type=F32
            )
        if with_taps:
            outer = jnp.dot(x_turned, jnp.concatenate(own_grad, axis=1), preferred_element_type=F32)
        for i in range(2):
            ch = 2 * pair + i
            if with_kv:
                keep_own(out, product, ch, i)
            if with_taps:
                cols = slice(i * 128, (i + 1) * 128)
                both = jnp.where(lane_at >= row_at, outer[128:, cols], outer[:128, cols])
                acc = both[0:8]
                for v in range(1, 16):
                    acc = acc + pltpu.roll(both[8 * v : 8 * v + 8], 128 - 8 * v, 1)
                part[ch] = acc
    if with_kv:
        for b in range(8):
            kv_grad[rows, b * 128 : (b + 1) * 128] = jnp.concatenate(out[b], axis=0).astype(BF)
    if with_taps:
        taps_part = part[:, 0, :]
        for u in range(1, 8):
            taps_part = taps_part + pltpu.roll(part[:, u, :], 128 - u, 1)
        return taps_part


NCH = 2


def remote(src, dst, send, recv, **where):
    return pltpu.make_async_remote_copy(src, dst, send, recv, device_id=where, device_id_type=pl.DeviceIdType.MESH)


def exchange_kernel(
    g_ref, w_ref, gate_hbm, kv_hbm, filt_ref,
    gate_grad_ref, kv_grad_ref, filt_grad_ref, w_grad_ref,
    gbuf, wbuf, gated_t, prod, mix, head, after, tail, before, taps,
    gate, kv, mixed, work, part, fsum, fin,
    y1s, y1b, y2s, y2b, x1s, x1b, x2s, x2b, zs, zb,
    g_send, g_recv, s_send, s_recv, w_send, w_recv,
    y1_send, y1_recv, y2_send, y2_recv, x1_send, x1_recv, x2_send, x2_recv, z_send, z_recv,
    h_send, h_recv, b_send, b_recv, t_send, t_recv, f_send, f_recv, l_sem, *, scale,
):
    c = lax.axis_index("ctx")
    f = lax.axis_index("fsdp")
    z, k = f // 2, f % 2
    zh, x, y = c // 16, (c // 4) % 4, c % 4
    xy = c % 16
    right, left, twin = f + 2, f - 2, f + 1 - 2 * k
    partner = (c + 16) % 32

    def at_y(d):
        return c - y + (y + d) % 4

    def at_x(d):
        return c + 4 * ((x + d) % 4 - x)

    barrier = pltpu.get_barrier_semaphore()

    def greet(**where):
        pl.semaphore_signal(barrier, inc=1, device_id=where, device_id_type=pl.DeviceIdType.MESH)

    @pl.when(z < 3)
    def _():
        greet(fsdp=right)

    @pl.when(z > 0)
    def _():
        greet(fsdp=left)

    greet(fsdp=twin)

    def greet_peer(i, carry):
        greet(ctx=(c + i) % 32)
        return carry

    lax.fori_loop(1, 32, greet_peer, 0)
    own_g = pltpu.make_async_copy(g_ref, gbuf.at[f], l_sem.at[0])
    own_kv = pltpu.make_async_copy(kv_hbm, kv, l_sem.at[1])
    own_gate = pltpu.make_async_copy(gate_hbm, gate, l_sem.at[2])
    own_kv.start()
    own_g.start()
    own_gate.start()
    turned = w_ref[...].astype(F32).T.astype(BF)
    home = (xy, 4 * y + x)
    for h in range(2):
        wbuf[h, home[h], zh] = turned[256 * h : 256 * h + 256]
    taps[c] = filt_ref[...]
    own_kv.wait()
    tail[...] = kv[:, 896:]

    @pl.when(c == 0)
    def _():
        before[...] = jnp.zeros_like(before)

    @pl.when(c == 31)
    def _():
        after[...] = jnp.zeros_like(after)

    count = jnp.where(z < 3, 1, 0) + jnp.where(z > 0, 1, 0) + 32
    pl.semaphore_wait(barrier, count)
    own_g.wait()

    span = 512 // NCH

    def g_copy(p, ch, way):
        block = gbuf.at[2 * p + k, pl.ds(ch * span, span)]
        return remote(block, block, g_send.at[p, ch, way], g_recv.at[p, ch], fsdp=right - 4 * way)

    def twin_copy(p, ch):
        block = gbuf.at[2 * p + k, pl.ds(ch * span, span)]
        return remote(block, block, s_send, s_recv.at[p, ch], fsdp=twin)

    across, along = (at_y, at_x), (at_x, at_y)
    line = (x, y)

    def w_remote(block, n, to):
        return remote(block, block, w_send.at[n], w_recv.at[n], ctx=to)

    def wz_copy(h):
        return w_remote(wbuf.at[h, home[h], zh], h, partner)

    def w1_copy(h, d):
        return w_remote(wbuf.at[h, home[h]], 2 + 4 * h + d, across[h](d))

    def w2_copy(h, d):
        return w_remote(wbuf.at[h, pl.ds(4 * line[h], 4)], 10 + 4 * h + d, along[h](d))

    def w3_copy(h, d):
        first = 4 * ((line[h] - d) % 4) + (0 if d == 1 else 2)
        return w_remote(wbuf.at[h, pl.ds(first, 2)], 18 + 4 * h + d, along[h](d))

    for h in range(2):
        wz_copy(h).start()

    def b_copy():
        return remote(tail, before, b_send, b_recv, ctx=c + 1)

    def t_copy(i):
        block = taps.at[c]
        return remote(block, block, t_send, t_recv, ctx=(c + i) % 32)

    def t_all():
        return remote(taps.at[pl.ds(0, 31)], taps.at[pl.ds(0, 31)], t_send, t_recv, ctx=partner)

    def send_taps(i, carry):
        t_copy(i).start()
        return carry

    lax.fori_loop(1, 32, send_taps, 0)

    @pl.when(c < 31)
    def _():
        b_copy().start()

    for ch in range(NCH):
        @pl.when(z < 3)
        def _():
            g_copy(z, ch, 0).start()

        @pl.when(z > 0)
        def _():
            g_copy(z, ch, 1).start()

        twin_copy(z, ch).start()

    mix[...] = jnp.zeros_like(mix)

    for h in range(2):
        wz_copy(h).wait_recv()
        for d in (1, 3, 2):
            w1_copy(h, d).start()
    t_all().wait_recv()

    @pl.when(c > 0)
    def _():
        b_copy().wait_recv()

    own_gate.wait()

    def filter_forward(g, carry):
        rows = pl.ds(pl.multiple_of(g * 16, 16), 16)
        xs = [before[rows, :]] + [kv[rows, b * 128 : (b + 1) * 128] for b in range(8)]
        lhs = jnp.concatenate([jnp.concatenate([xs[b], xs[b + 1]], axis=1) for b in range(8)], axis=0)
        outs = conv_group(taps[g].astype(F32), lhs, False)
        for b in range(8):
            cols = slice(b * 128, (b + 1) * 128)
            narrow = outs[b].astype(BF)
            mixed[rows, cols] = narrow
            work[rows, cols] = (gate[rows, cols].astype(F32) * narrow.astype(F32)).astype(BF)
        return carry

    def sides(s, act):
        if s == 0:
            act(z)
            return

        def one(side, carry):
            p = z - s + 2 * s * side

            @pl.when((p >= 0) & (p < 4))
            def _():
                act(p)

            return carry

        lax.fori_loop(0, 2, one, 0)

    def pass_on(s, ch):
        def act(p):
            g_copy(p, ch, 0).wait_recv()

            @pl.when((p < z) & (z < 3))
            def _():
                g_copy(p, ch, 0).start()

            @pl.when((p > z) & (z > 0))
            def _():
                g_copy(p, ch, 1).start()

            twin_copy(p, ch).start()

        sides(s, act)

    lax.fori_loop(0, 8, filter_forward, 0, unroll=2)
    for h in range(2):
        for d in (1, 3, 2):
            w1_copy(h, d).wait_recv()
        for d in (1, 3):
            w2_copy(h, d).start()
    lax.fori_loop(8, 20, filter_forward, 0, unroll=2)
    pass_on(1, 0)
    lax.fori_loop(20, 32, filter_forward, 0, unroll=2)

    def turn(i, carry):
        cols = pl.ds(pl.multiple_of(i * 128, 128), 128)
        gated_t[:, cols] = work[cols, :].astype(F32).T.astype(BF)
        return carry

    lax.fori_loop(0, 4, turn, 0)

    def y1_copy(b, j):
        return remote(y1s.at[b, j], y1b.at[b, j], y1_send, y1_recv.at[b, j], ctx=at_y(1 if j == 0 else 3))

    def y2_copy(b, j):
        return remote(y2s.at[b, j], y2b.at[b, j], y2_send, y2_recv.at[b, j], ctx=at_y(1 if j == 0 else 3))

    def x1_copy(b, j):
        return remote(x1s.at[b, j], x1b.at[b, j], x1_send, x1_recv.at[b, j], ctx=at_x(1 if j == 0 else 3))

    def x2_copy(b, j):
        return remote(x2s.at[b], x2b.at[b, j], x2_send, x2_recv.at[b, j], ctx=at_x(1 if j == 0 else 3))

    def z_copy():
        return remote(zs, zb, z_send, z_recv, ctx=partner)

    def multiply_rows(p):
        def tile(i, carry):
            b, h = 2 * p + i // 2, i % 2
            lhs = gbuf[b, pl.ds(pl.multiple_of(h * 256, 256), 256), :]
            part = jnp.dot(lhs, gated_t[...], preferred_element_type=F32)
            prod[b, pl.ds(2 * h, 2)] = part.reshape(2, 128, 512)
            return carry

        lax.fori_loop(0, 4, tile, 0)
        for i in range(2):
            b = 2 * p + i
            far = prod[b, (y + 2) % 4].astype(BF)
            y1s[b, 0] = far[:, :256]
            y1s[b, 1] = far[:, 256:]
            for j in range(2):
                y1_copy(b, j).start()

    def multiply_columns(p):
        for h in range(2):
            rows = slice(256 * h, 256 * h + 256)

            def tile(n, carry):
                cols = pl.ds(pl.multiple_of(n * 512, 512), 512)
                slabs = []
                for e in range(8):
                    row, q = (2 * p + e // 4) % 4, e % 4
                    slabs.append(wbuf[h, 4 * row + q if h == 0 else 4 * q + row, p // 2])
                rhs = gbuf[pl.ds(2 * p, 2), :, cols].reshape(1024, 512)
                mix[rows, cols] += jnp.dot(jnp.concatenate(slabs, axis=1), rhs, preferred_element_type=F32)
                return carry

            lax.fori_loop(0, 2, tile, 0)

    def round_y2(p):
        for i in range(2):
            b = 2 * p + i
            y1_copy(b, 0).wait_recv()
            up = prod[b, (y + 1) % 4]
            y2s[b, 0, :, :256] = (up[:, :256] + y1b[b, 0].astype(F32)).astype(BF)
            y2s[b, 0, :, 256:] = up[:, 256:].astype(BF)
            y2_copy(b, 0).start()
            y1_copy(b, 1).wait_recv()
            down = prod[b, (y + 3) % 4]
            y2s[b, 1, :, :256] = down[:, :256].astype(BF)
            y2s[b, 1, :, 256:] = (down[:, 256:] + y1b[b, 1].astype(F32)).astype(BF)
            y2_copy(b, 1).start()

    def round_x1(p):
        for i in range(2):
            b = 2 * p + i
            y2_copy(b, 0).wait_recv()
            y2_copy(b, 1).wait_recv()
            total = prod[b, y] + y2b[b, 0].astype(F32) + y2b[b, 1].astype(F32)
            prod[b, y] = total

            @pl.when((x - b) % 4 == 2)
            def _():
                x1s[b, 0] = total[:, :256].astype(BF)
                x1s[b, 1] = total[:, 256:].astype(BF)
                for j in range(2):
                    x1_copy(b, j).start()

    def round_x2(p):
        for i in range(2):
            b = 2 * p + i
            role = (x - b) % 4

            @pl.when(role == 3)
            def _():
                x1_copy(b, 0).wait_recv()
                x2s[b, :, :256] = (prod[b, y, :, :256] + x1b[b, 0].astype(F32)).astype(BF)
                x2s[b, :, 256:] = prod[b, y, :, 256:].astype(BF)
                x2_copy(b, 0).start()

            @pl.when(role == 1)
            def _():
                x1_copy(b, 1).wait_recv()
                x2s[b, :, :256] = prod[b, y, :, :256].astype(BF)
                x2s[b, :, 256:] = (prod[b, y, :, 256:] + x1b[b, 1].astype(F32)).astype(BF)
                x2_copy(b, 1).start()

    def round_z(p):
        for i in range(2):
            b = 2 * p + i

            @pl.when((x - b) % 4 == 0)
            def _():
                x2_copy(b, 0).wait_recv()
                x2_copy(b, 1).wait_recv()
                total = prod[b, y] + x2b[b, 0].astype(F32) + x2b[b, 1].astype(F32)

                @pl.when(b // 4 == zh)
                def _():
                    prod[b, y] = total

                @pl.when(b // 4 != zh)
                def _():
                    zs[...] = total.astype(BF)
                    z_copy().start()

    def arrive(p):
        for ch in range(NCH):
            twin_copy(p, ch).wait_recv()
        multiply_rows(p)

    arrive(z)
    pass_on(1, 1)
    for h in range(2):
        for d in (1, 3):
            w2_copy(h, d).wait_recv()
            w3_copy(h, d).start()
    sides(0, round_y2)
    sides(1, arrive)
    pass_on(2, 0)
    sides(0, round_x1)
    sides(1, round_y2)
    pass_on(2, 1)
    sides(0, round_x2)
    sides(2, arrive)
    sides(1, round_x1)
    pass_on(3, 0)
    sides(2, round_y2)
    sides(1, round_x2)
    for h in range(2):
        for d in (1, 3):
            w3_copy(h, d).wait_recv()
    for s in (0, 1, 2):
        sides(s, multiply_columns)
    sides(2, round_x1)
    pass_on(3, 1)
    sides(3, arrive)
    sides(3, multiply_columns)

    def h_copy():
        return remote(head, after, h_send, h_recv, ctx=c - 1)

    def finish_head(i, carry):
        rows = pl.ds(pl.multiple_of(i * 64, 64), 64)
        head[rows, :] = (mix[rows, :128] * gate[rows, :128].astype(F32)).astype(BF)
        return carry

    lax.fori_loop(0, 8, finish_head, 0)

    @pl.when(c > 0)
    def _():
        h_copy().start()

    def finish(i, carry):
        rows = pl.ds(pl.multiple_of(i * 32, 32), 32)
        wide = mix[rows, :]
        work[rows, :] = (wide * gate[rows, :].astype(F32)).astype(BF)
        mix[rows, :] = wide * mixed[rows, :].astype(F32)
        return carry

    lax.fori_loop(0, 16, finish, 0)
    out_gate = pltpu.make_async_copy(mix, gate_grad_ref, l_sem.at[3])
    out_gate.start()
    sides(3, round_y2)
    sides(2, round_x2)

    def f_copy(i):
        return remote(fsum.at[(c + i) % 32], fin.at[i], f_send, f_recv, ctx=(c + i) % 32)

    def f_all():
        return remote(fsum.at[pl.ds(0, 31)], fin.at[pl.ds(1, 31)], f_send, f_recv, ctx=partner)

    def filter_back(i, with_kv, with_taps):
        g = (c + i) % 32
        rows = pl.ds(pl.multiple_of(g * 16, 16), 16)
        total = back_group(
            before, kv, work, after, rows, taps[g].astype(F32), part, kv_grad_ref, with_kv, with_taps
        )
        if with_taps:
            fsum[g] = total

            @pl.when(i < 32)
            def _():
                f_copy(i).start()

        return 0

    lax.fori_loop(1, 9, lambda i, carry: filter_back(i, False, True), 0, unroll=2)
    sides(3, round_x1)

    @pl.when(c < 31)
    def _():
        h_copy().wait_recv()

    lax.fori_loop(9, 17, lambda i, carry: filter_back(i, True, True), 0, unroll=2)
    sides(3, round_x2)
    for s in (0, 1, 2):
        sides(s, round_z)
    lax.fori_loop(17, 25, lambda i, carry: filter_back(i, True, True), 0, unroll=2)
    sides(3, round_z)
    lax.fori_loop(25, 33, lambda i, carry: filter_back(i, True, True), 0, unroll=2)
    lax.fori_loop(1, 9, lambda i, carry: filter_back(i, True, False), 0, unroll=2)
    z_copy().wait_recv()
    w_grad_ref[...] = (prod[4 * zh + x, y] + zb[...].astype(F32)) * scale
    f_all().wait_recv()
    total = fsum[c]
    for i in range(1, 32):
        total = total + fin[i]
    filt_grad_ref[...] = total * scale
    out_gate.wait()

    def sent_blocks(p, carry):
        for ch in range(NCH):
            @pl.when((p <= z) & (z < 3))
            def _():
                g_copy(p, ch, 0).wait_send()

            @pl.when((p >= z) & (z > 0))
            def _():
                g_copy(p, ch, 1).wait_send()

        return carry

    lax.fori_loop(0, 4, sent_blocks, 0)

    def left(src, sem):
        remote(src, src, sem, sem, ctx=partner).wait_send()

    left(gbuf.at[pl.ds(0, 4)], s_send)
    left(y1s, y1_send)
    left(y2s, y2_send)
    left(x1s.at[pl.ds(0, 2)], x1_send)
    left(x2s.at[pl.ds(0, 4)], x2_send)
    z_copy().wait_send()
    for h in range(2):
        wz_copy(h).wait_send()
        for d in (1, 2, 3):
            w1_copy(h, d).wait_send()
        for d in (1, 3):
            w2_copy(h, d).wait_send()
            w3_copy(h, d).wait_send()

    @pl.when(c > 0)
    def _():
        h_copy().wait_send()

    @pl.when(c < 31)
    def _():
        b_copy().wait_send()

    t_all().wait_send()
    f_all().wait_send()


def exchange(out_grad, w_out, gate, kv, filters, scale):
    vmem = pl.BlockSpec(memory_space=pltpu.VMEM)
    hbm = pl.BlockSpec(memory_space=pl.ANY)
    dma = pltpu.SemaphoreType.DMA
    return pl.pallas_call(
        functools.partial(exchange_kernel, scale=scale),
        out_shape=[
            jax.ShapeDtypeStruct((512, 1024), F32),
            jax.ShapeDtypeStruct((512, 1024), BF),
            jax.ShapeDtypeStruct((16, 128), F32),
            jax.ShapeDtypeStruct((128, 512), F32),
        ],
        in_specs=[hbm, vmem, hbm, hbm, vmem],
        out_specs=[hbm, vmem, vmem, vmem],
        scratch_shapes=[
            pltpu.VMEM((8, 512, 1024), BF),
            pltpu.VMEM((2, 16, 2, 256, 128), BF),
            pltpu.VMEM((1024, 512), BF),
            pltpu.VMEM((8, 4, 128, 512), F32),
            pltpu.VMEM((512, 1024), F32),
            pltpu.VMEM((512, 128), BF),
            pltpu.VMEM((512, 128), BF),
            pltpu.VMEM((512, 128), BF),
            pltpu.VMEM((512, 128), BF),
            pltpu.VMEM((32, 16, 128), BF),
            pltpu.VMEM((512, 1024), BF),
            pltpu.VMEM((512, 1024), BF),
            pltpu.VMEM((512, 1024), BF),
            pltpu.VMEM((512, 1024), BF),
            pltpu.VMEM((16, 8, 128), F32),
            pltpu.VMEM((32, 16, 128), F32),
            pltpu.VMEM((32, 16, 128), F32),
            pltpu.VMEM((8, 2, 128, 256), BF),
            pltpu.VMEM((8, 2, 128, 256), BF),
            pltpu.VMEM((8, 2, 128, 512), BF),
            pltpu.VMEM((8, 2, 128, 512), BF),
            pltpu.VMEM((8, 2, 128, 256), BF),
            pltpu.VMEM((8, 2, 128, 256), BF),
            pltpu.VMEM((8, 128, 512), BF),
            pltpu.VMEM((8, 2, 128, 512), BF),
            pltpu.VMEM((128, 512), BF),
            pltpu.VMEM((128, 512), BF),
            dma((4, NCH, 2)), dma((4, NCH)), dma, dma((4, NCH)), dma((26,)), dma((26,)),
            dma, dma((8, 2)), dma, dma((8, 2)), dma, dma((8, 2)), dma, dma((8, 2)),
            dma, dma, dma, dma, dma, dma, dma, dma, dma, dma, dma((4,)),
        ],
        compiler_params=pltpu.CompilerParams(
            collective_id=0, has_side_effects=True, vmem_limit_bytes=60 << 20
        ),
    )(out_grad, w_out, gate, kv, filters)


def on_device(out_grad, gate_values, kv_product, w_out, filters):
    scale = 1.0 / math.sqrt(lax.axis_size("ctx") * out_grad.shape[1])
    gate_grad, kv_grad, filter_grad, w_grad = exchange(
        out_grad, w_out, gate_values, kv_product, filters.reshape(filters.shape[2:]), scale
    )
    return (gate_grad, kv_grad, filter_grad.reshape(filters.shape), w_grad)


def solution(mesh):
    in_specs = (
        P("fsdp", "ctx"),
        P("fsdp", "ctx"),
        P("fsdp", "ctx"),
        P("ctx", "fsdp"),
        P("fsdp", "ctx", None, None),
    )
    out_specs = (P("fsdp", "ctx"), P("fsdp", "ctx"), P("fsdp", "ctx", None, None), P("ctx", "fsdp"))
    return jax.shard_map(
        on_device, mesh=mesh, in_specs=in_specs, out_specs=out_specs, check_vma=False
    )
```
